128 devices in a mesh: gx: 8 (over y_lo, z), gy: 16 (over y_hi, x, core).
Axes of the slice: x: 4, y: 4 (y_hi: 2, y_lo: 2; y = y_hi * 2 + y_lo), z: 4, core: 2. Of those that a mesh axis runs over, the one named last changes fastest.
Arguments:
- features: bfloat16 [64, 256, 16, 128], P('gx', 'gy'), may hold values from -6 to 6
- w_first: bfloat16 [27, 128, 128], replicated, may hold values from -0.109375 to 0.109375
- w_second: bfloat16 [27, 128, 128], replicated, may hold values from -0.109375 to 0.109375
- occupancy: int32 [8, 32, 2], P('gx', 'gy'), may hold values from 0 to 1, as said below
- cotangent: bfloat16 [64, 256, 16, 128], P('gx', 'gy'), may hold values from -6 to 6
Outputs:
- output: bfloat16 [64, 256, 16, 128], P('gx', 'gy')
- grad_features: bfloat16 [64, 256, 16, 128], P('gx', 'gy')
- grad_first: float32 [27, 128, 128], P(None, 'gy')
- grad_second: float32 [27, 128, 128], P(None, 'gy')
The draws below stay inside these ranges and needn't reach their ends.
Inputs may be any that keep to these rules, and one draw needn't show every extreme that they name: `occupancy`: 1 marks an active block; the share of active blocks differs from one tile of 1 x 2 x 2 blocks to another.
All inputs are finite; a program needn't handle non-finite values.
Results may differ from the reference program's by a relative error of at most 0.0025.
The reference program's roundings to bfloat16 on the way (of `active`, `masked`, `hidden`, `up_grad` and `pre_grad`) count: a program that leaves them out, or rounds other values in their place, can miss the bound.
Values may be sent and summed in bfloat16 or wider, within the bound.
A program may use at most 128 MiB of HBM per device.

```python
import math
import jax
import jax.numpy as jnp
from jax import lax

C = 128
TBX = 1
TBY = 2
NX = 64
NY = 256
NZ = 16
NBX = 8
NBY = 32
NBZ = 2


def draw_occupancy(key, part):
    base = jax.random.fold_in(key, 4471)
    key_tiles, key_blocks = jax.random.split(base)
    tiles_x = NBX // TBX
    tiles_y = NBY // TBY
    density = jax.random.randint(key_tiles, (tiles_x, tiles_y), 5, 101)
    spread = jnp.repeat(jnp.repeat(density, TBX, axis=0), TBY, axis=1)[:, :, None]
    rolled = jax.random.randint(key_blocks, (NBX, NBY, NBZ), 0, 100)
    return (rolled < spread).astype(jnp.int32)


def level_of(own_key, extent, cuts, smallest, high):
    loudness = 1.0
    for dim, shards_of in cuts:
        heights = jax.random.uniform(jax.random.fold_in(jax.random.fold_in(own_key, 6), dim), (shards_of,), jnp.float32, smallest / len(cuts), high / len(cuts))
        loudness = loudness * jnp.repeat(jnp.exp(heights), extent[dim] // shards_of).reshape((-1,) + (1,) * (len(extent) - 1 - dim))
    return loudness


def scatter_about(rng, dims, deviation, limit, cuts=(), held_as=jnp.bfloat16):
    array = jax.random.normal(rng, dims, jnp.float32) * deviation
    if len(cuts) > 0:
        array = level_of(rng, dims, cuts, -0.22, 0.18) * array
    return jnp.clip(array, min=-limit, max=limit).astype(held_as)


def setup_inputs(seed: int = 0) -> dict:
    key_of = jax.random.split(jax.random.key(seed), 6)
    return {
        "features": scatter_about(key_of[0], (NX, NY, NZ, C), 1.0, 6.0, ((0, 8), (1, 16))),
        "w_first": scatter_about(key_of[1], (27, C, C), (27 * C) ** -0.5, 0.109375),
        "w_second": scatter_about(key_of[2], (27, C, C), (27 * C) ** -0.5, 0.109375),
        "occupancy": draw_occupancy(jax.random.fold_in(key_of[5], 71), 0),
        "cotangent": scatter_about(key_of[4], (NX, NY, NZ, C), 1.0, 6.0, ((0, 8), (1, 16))),
    }


def voxel_mask(occupancy):
    block_x, block_y, block_z = occupancy.shape
    spread = jnp.broadcast_to(occupancy[:, None, :, None, :, None], (block_x, 8, block_y, 8, block_z, 8))
    return spread.reshape(block_x * 8, block_y * 8, block_z * 8).astype(jnp.bfloat16)

def arrange(weights):
    channels = weights.shape[2]
    forward = weights.reshape(3, 9 * channels, channels)
    backward = weights.reshape(3, 3, 3, channels, channels).swapaxes(3, 4).reshape(3, 9 * channels, channels)
    return (forward, backward)

def shifted_rows(padded, plane_x, flipped):
    inner_x = padded.shape[0] - 2
    inner_y = padded.shape[1] - 2
    inner_z = padded.shape[2] - 2
    channels = padded.shape[3]
    pieces = []
    for step_y in range(3):
        for step_z in range(3):
            if flipped:
                anchor = (2 - plane_x, 2 - step_y, 2 - step_z)
            else:
                anchor = (plane_x, step_y, step_z)
            pieces.append(padded[anchor[0]:anchor[0] + inner_x, anchor[1]:anchor[1] + inner_y, anchor[2]:anchor[2] + inner_z])
    return jnp.concatenate(pieces, axis=3).reshape(inner_x * inner_y * inner_z, 9 * channels)

def convolve(padded, kernel, flipped):
    inner_x = padded.shape[0] - 2
    inner_y = padded.shape[1] - 2
    inner_z = padded.shape[2] - 2
    summed = jnp.zeros((inner_x * inner_y * inner_z, kernel.shape[2]), jnp.float32)
    for plane_x in range(3):
        summed = summed + jnp.dot(shifted_rows(padded, plane_x, flipped), kernel[plane_x], preferred_element_type=jnp.float32)
    return summed.reshape(inner_x, inner_y, inner_z, kernel.shape[2])

def kernel_grad(padded, upstream):
    channels = upstream.shape[3]
    grad_rows = upstream.reshape(-1, channels)
    planes = []
    for plane_x in range(3):
        planes.append(lax.dot_general(shifted_rows(padded, plane_x, False), grad_rows, (((0,), (0,)), ((), ())), preferred_element_type=jnp.float32))
    return jnp.stack(planes).reshape(27, channels, channels)

def pad_all(field):
    return jnp.pad(field, ((1, 1), (1, 1), (1, 1), (0, 0)))

def slab_convolve(padded, kernel, flipped):
    slab_count = (padded.shape[0] - 2) // 8

    def per_slab(number):
        window = lax.dynamic_slice_in_dim(padded, number * 8, 10, 0)
        return convolve(window, kernel, flipped)
    stacked = lax.map(per_slab, jnp.arange(slab_count, dtype=jnp.int32))
    return stacked.reshape((-1,) + stacked.shape[2:])

def slab_kernel_grad(padded, upstream):
    slab_count = upstream.shape[0] // 8
    channels = upstream.shape[3]

    def accumulate(carried, number):
        window = lax.dynamic_slice_in_dim(padded, number * 8, 10, 0)
        grad_window = lax.dynamic_slice_in_dim(upstream, number * 8, 8, 0)
        return (carried + kernel_grad(window, grad_window), None)
    start_value = jnp.zeros((27, channels, channels), jnp.float32)
    result, unused = lax.scan(accumulate, start_value, jnp.arange(slab_count, dtype=jnp.int32))
    return result

def reference(features, w_first, w_second, occupancy, cotangent):
    active = voxel_mask(occupancy)[..., None]
    active_f = active.astype(jnp.float32)
    masked = features * active
    first_fwd, first_bwd = arrange(w_first)
    second_fwd, second_bwd = arrange(w_second)
    padded_x = pad_all(masked)
    pre_act = slab_convolve(padded_x, first_fwd, False)
    hidden = (active_f * jax.nn.silu(pre_act)).astype(jnp.bfloat16)
    padded_hidden = pad_all(hidden)
    second = slab_convolve(padded_hidden, second_fwd, False)
    output = (masked.astype(jnp.float32) + active_f * second).astype(jnp.bfloat16)
    up_grad = cotangent * active
    hidden_grad = slab_convolve(pad_all(up_grad), second_bwd, True)
    sigmoid_pre = jax.nn.sigmoid(pre_act)
    pre_grad = (active_f * hidden_grad * sigmoid_pre * (1.0 + pre_act * (1.0 - sigmoid_pre))).astype(jnp.bfloat16)
    feature_term = slab_convolve(pad_all(pre_grad), first_bwd, True)
    grad_features = (active_f * (cotangent.astype(jnp.float32) + feature_term)).astype(jnp.bfloat16)
    factor = 1.0 / math.sqrt(NX * NY * NZ)
    grad_second = slab_kernel_grad(padded_hidden, up_grad) * factor
    grad_first = slab_kernel_grad(padded_x, pre_grad) * factor
    return (output, grad_features, grad_first, grad_second)
```

```python
import functools
import math

import jax
import jax.numpy as jnp
from jax import lax
from jax.experimental import pallas as pl
from jax.experimental.pallas import tpu as pltpu
from jax.sharding import PartitionSpec as P

F32 = jnp.float32
BF16 = jnp.bfloat16
MESH = pl.DeviceIdType.MESH
DIRS = [(ax, ay) for ax in (-1, 0, 1) for ay in (-1, 0, 1) if (ax, ay) != (0, 0)]
GX, GY = 8, 16
X, Y, Z, C = 8, 16, 16, 128
TAPS = 28
ALL = [(0, 8, 0, 8)]
INNER = [(1, 6, 1, 6)]
RIM = [(0, 1, 0, 8), (7, 1, 0, 8), (1, 6, 0, 1), (1, 6, 7, 1)]


def kernel(
    scale,
    occ_ref, feat_hbm, cot_hbm, w1_hbm, w2_hbm,
    out_hbm, gf_hbm, g1_hbm, g2_hbm,
    feat, cot, w1, w2, fu, hq, slope, at, outs, part,
    r0, s0, r1a, r1b, r1c, a1, b1, c1, r2a, r2b, r2c, ab2, c2, r3, r3c, ab3, c3, r4, rc4, done,
    in_sem, out_sem, hs, hr, s0s, s0r, s1s, s1r, s2s, s2r, s3s, s3r, s4s, s4r,
):
    gx = lax.axis_index("gx")
    gy = lax.axis_index("gy")
    core = gy % 2
    px = (gy // 2) % 4
    yh = gy // 8
    pz = gx % 4
    yl = gx // 4
    py = yh * 2 + yl

    def at_x(k):
        return (px + k) % 4

    def at_y(k):
        return (py + k) % 4

    def at_z(k):
        return (pz + k) % 4

    def dev_x(k):
        return (gx, yh * 8 + at_x(k) * 2 + core)

    def dev_y(k):
        to = at_y(k)
        return ((to % 2) * 4 + pz, (to // 2) * 8 + px * 2 + core)

    def dev_z(k):
        return (yl * 4 + at_z(k), gy)

    partner = (gx, gy + 1 - 2 * core)

    def exists(ax, ay):
        ok = None
        for step, pos, size in ((ax, gx, GX), (ay, gy, GY)):
            if step == 0:
                continue
            here = pos + 1 < size if step > 0 else pos > 0
            ok = here if ok is None else jnp.logical_and(ok, here)
        return ok

    barrier = pltpu.get_barrier_semaphore()
    for ax, ay in DIRS:
        @pl.when(exists(ax, ay))
        def _():
            pl.semaphore_signal(barrier, inc=1, device_id=(gx + ax, gy + ay), device_id_type=MESH)
    fixed = [partner] + [dev_x(k) for k in (1, 2, 3)] + [dev_y(k) for k in (1, 2, 3)]
    fixed += [((gx + k) % GX, gy) for k in range(1, GX)]
    for peer in fixed:
        pl.semaphore_signal(barrier, inc=1, device_id=peer, device_id_type=MESH)

    loads = [
        pltpu.make_async_copy(src, dst, in_sem.at[i])
        for i, (src, dst) in enumerate(
            ((feat_hbm, feat), (cot_hbm, cot), (w1_hbm, w1), (w2_hbm, w2))
        )
    ]
    for load in loads:
        load.start()

    low = lax.broadcasted_iota(jnp.int32, (Z, C), 0) < 8
    mask = [
        jnp.where(low, occ_ref[0, b, 0].astype(F32), occ_ref[0, b, 1].astype(F32)) for b in range(2)
    ]

    def mask_rows(boxes, wide):
        rows = []
        for x0, nx, k0, nk in boxes:
            for _ in range(nx):
                rows += [mask[k // 4] for k in range(k0, k0 + nk)]
        m = jnp.concatenate(rows, axis=0)
        return jnp.concatenate([m, m], axis=1) if wide else m

    def z_shift(field, at_index):
        v = field[(1, *at_index)].astype(F32)
        n = math.prod(v.shape[:-1])
        t = v.reshape(n, C)
        z = lax.broadcasted_iota(jnp.int32, (n, C), 0) % Z
        down = jnp.where(z == 0, 0.0, pltpu.roll(t, 1, 0))
        up = jnp.where(z == Z - 1, 0.0, pltpu.roll(t, n - 1, 0))
        field[(0, *at_index)] = down.astype(BF16).reshape(v.shape)
        field[(2, *at_index)] = up.astype(BF16).reshape(v.shape)

    def edge_x(step, recv):
        if step == 0:
            return (pl.ds(1, X),)
        if recv:
            return (0 if step > 0 else X + 1,)
        return (X if step > 0 else 1,)

    def edge_y(step, recv):
        if step == 0:
            return (pl.ds(1, 8),)
        if recv:
            return (0, 1) if step > 0 else (9, 0)
        return (8, 1) if step > 0 else (1, 0)

    def halo_copy(ref, d, slot):
        ax, ay = DIRS[d]
        lead = (1,) if len(ref.shape) == 6 else (slice(None), 1)
        return pltpu.make_async_remote_copy(
            src_ref=ref.at[(*lead, *edge_x(ax, False), *edge_y(ay, False))],
            dst_ref=ref.at[(*lead, *edge_x(ax, True), *edge_y(ay, True))],
            send_sem=hs.at[slot, d],
            recv_sem=hr.at[slot, d],
            device_id=(gx + ax, gy + ay),
            device_id_type=MESH,
        )

    def halo_start(ref, slot):
        for d, (ax, ay) in enumerate(DIRS):
            @pl.when(exists(ax, ay))
            def _():
                halo_copy(ref, d, slot).start()

    def halo_zero(ref):
        lead = (1,) if len(ref.shape) == 6 else (slice(None), 1)
        for ax, ay in DIRS:
            @pl.when(jnp.logical_not(exists(-ax, -ay)))
            def _():
                index = (*lead, *edge_x(ax, True), *edge_y(ay, True))
                ref[index] = jnp.zeros(ref.at[index].shape, BF16)

    def halo_wait(ref, slot):
        for d, (ax, ay) in enumerate(DIRS):
            @pl.when(exists(-ax, -ay))
            def _():
                halo_copy(ref, d, slot).wait_recv()

    def halo_sent(ref, slot):
        for d, (ax, ay) in enumerate(DIRS):
            @pl.when(exists(ax, ay))
            def _():
                halo_copy(ref, d, slot).wait_send()

    def shift_rim(field):
        for x in (0, X + 1):
            z_shift(field, (x,))
        for edge in ((0, 1), (9, 0)):
            z_shift(field, (pl.ds(1, X), *edge))

    def shift_inner(field):
        for x in range(1, X + 1):
            z_shift(field, (x, pl.ds(1, 8)))

    def rows_of(field, boxes, dz, dx, j):
        halves = []
        for h in range(2):
            pieces = [
                field[dz, pl.ds(x0 + dx, nx), pl.ds(k0 + j + h, nk), 1 - h].reshape(nx * nk * Z, C)
                for x0, nx, k0, nk in boxes
            ]
            halves.append(jnp.concatenate(pieces, axis=0) if len(pieces) > 1 else pieces[0])
        return jnp.concatenate(halves, axis=1)

    zero = jnp.zeros((C, C), BF16)

    def conv(field, w, boxes, flipped):
        left, right = [], []
        for dx in range(3):
            for dz in range(3):
                tap = [w[26 - (9 * dx + 3 * dy + dz)] if flipped else w[9 * dx + 3 * dy + dz] for dy in range(3)]
                for j in range(2):
                    left.append(rows_of(field, boxes, dz, dx, j))
                    if j == 0:
                        grid = ((tap[0], zero), (tap[1], tap[0]))
                    else:
                        grid = ((tap[2], tap[1]), (zero, tap[2]))
                    if flipped:
                        grid = tuple(zip(*grid))
                        right.append(jnp.concatenate([jnp.concatenate(r, axis=1) for r in grid], axis=0))
                    else:
                        right.append(jnp.concatenate([jnp.concatenate(r, axis=1) for r in grid], axis=0))
        lhs = jnp.concatenate(left, axis=1)
        if flipped:
            return lax.dot_general(
                lhs, jnp.concatenate(right, axis=1), (((1,), (1,)), ((), ())), preferred_element_type=F32
            )
        return jnp.dot(lhs, jnp.concatenate(right, axis=0), preferred_element_type=F32)

    def tiles(boxes):
        at_row = 0
        for x0, nx, k0, nk in boxes:
            n = nx * nk * Z
            yield (x0, nx, k0, nk), slice(at_row, at_row + n)
            at_row += n

    def put(field_at, boxes, value):
        for (x0, nx, k0, nk), rows in tiles(boxes):
            for h in range(2):
                field_at(x0, nx, k0, nk, h, value[rows, h * C : (h + 1) * C].reshape(nx, nk, Z, C))

    def put_padded(field):
        def store(x0, nx, k0, nk, h, v):
            field[1, pl.ds(x0 + 1, nx), pl.ds(k0 + 1, nk), h] = v.astype(BF16)
        return store

    def forward(boxes):
        pre = conv(fu.at[0], w1, boxes, False)
        s = jax.nn.sigmoid(pre)
        m = mask_rows(boxes, True)
        put(put_padded(hq.at[0]), boxes, m * (pre * s))
        d = m * (s * (1.0 + pre * (1.0 - s)))
        for (x0, nx, k0, nk), rows in tiles(boxes):
            slope[pl.ds(x0, nx), pl.ds(k0, nk)] = d[rows].reshape(nx, nk, Z, 2 * C)

    def backward(boxes):
        grad = conv(fu.at[1], w2, boxes, True)
        d = [slope[pl.ds(x0, nx), pl.ds(k0, nk)].reshape(nx * nk * Z, 2 * C) for x0, nx, k0, nk in boxes]
        d = jnp.concatenate(d, axis=0) if len(d) > 1 else d[0]
        put(put_padded(hq.at[1]), boxes, grad * d)

    def finish(slot, w, flipped, boxes):
        acc = conv(hq.at[slot], w, boxes, flipped) * mask_rows(boxes, True)
        base = fu.at[slot]

        def store(x0, nx, k0, nk, h, v):
            b = base[1, pl.ds(x0 + 1, nx), pl.ds(k0 + 1, nk), h].astype(F32)
            outs[slot, pl.ds(x0, nx), pl.ds(k0, nk), h] = (b + v).astype(BF16)
        put(store, boxes, acc)

    def wgrad(g, left, right, mirrored):
        for h in range(2):
            for x in range(X):
                at[h, x] = left[1, x + 1, pl.ds(1, 8), h].reshape(8 * Z, C).T
        lhs = jnp.concatenate([at[h, x] for h in range(2) for x in range(X)], axis=1)

        @pl.loop(0, 3)
        def _(dx):
            cols = []
            for t in range(9):
                dy, dz = t // 3, t % 3
                ex, ey, ez = (2 - dx, 2 - dy, 2 - dz) if mirrored else (dx, dy, dz)
                halves = []
                for h in range(2):
                    row = h + ey + 1
                    halves.append(right[ez, pl.ds(ex, X), pl.ds(row // 2, 8), row % 2].reshape(X * 8 * Z, C))
                cols.append(jnp.concatenate(halves, axis=0))
            rhs = jnp.concatenate(cols, axis=1)
            acc = jnp.dot(lhs, rhs, preferred_element_type=F32)
            for t in range(9):
                block = acc[:, t * C : (t + 1) * C]
                if not mirrored:
                    block = block.T
                for s in range(16):
                    part[g, s % 2, (s // 2) % 4, s // 8, 9 * dx + t] = block[8 * s : 8 * s + 8]

    def remote(src, dst, send, recv, to):
        return pltpu.make_async_remote_copy(
            src_ref=src, dst_ref=dst, send_sem=send, recv_sem=recv, device_id=to, device_id_type=MESH
        )

    def stage0(g):
        return [remote(part.at[g, 1 - core], r0.at[g], s0s.at[g], s0r.at[g], partner)]

    def stage1(g):
        copies = []
        for k in (1, 2, 3):
            to = at_y(k)
            three = (
                (s0.at[g, at_x(k), :, pl.ds(0, 10)], r1a.at[g, k - 1], dev_x(k)),
                (s0.at[g, :, to // 2, pl.ds(10 + 5 * (to % 2), 5)], r1b.at[g, k - 1], dev_y(k)),
                (s0.at[g, :, :, pl.ds(20 + 2 * at_z(k), 2)], r1c.at[g, k - 1], dev_z(k)),
            )
            for i, (src, dst, dev) in enumerate(three):
                copies.append(remote(src, dst, s1s.at[g, i, k - 1], s1r.at[g, i, k - 1], dev))
        return copies

    def stage2(g):
        copies = []
        for k in (1, 2, 3):
            to = at_y(k)
            three = (
                (a1.at[g, to // 2, pl.ds(5 * (to % 2), 5)], r2a.at[g, k - 1], dev_y(k)),
                (b1.at[g, at_x(k)], r2b.at[g, k - 1], dev_x(k)),
                (c1.at[g, at_x(k)], r2c.at[g, k - 1], dev_x(k)),
            )
            for i, (src, dst, dev) in enumerate(three):
                copies.append(remote(src, dst, s2s.at[g, i, k - 1], s2r.at[g, i, k - 1], dev))
        return copies

    def stage3(g):
        copies = []
        for k in (1, 2, 3):
            to = at_y(k)
            two = (
                (ab2.at[g], r3.at[g, k - 1], dev_z(k)),
                (c2.at[g, to // 2, to % 2], r3c.at[g, k - 1], dev_y(k)),
            )
            for i, (src, dst, dev) in enumerate(two):
                copies.append(remote(src, dst, s3s.at[g, i, k - 1], s3r.at[g, i, k - 1], dev))
        return copies

    def stage4(g):
        copies = [remote(ab3.at[g], r4.at[g], s4s.at[g, 0], s4r.at[g, 0], ((gx + 4) % GX, gy))]
        for k in range(1, GX):
            copies.append(
                remote(c3.at[g], rc4.at[g, k - 1], s4s.at[g, k], s4r.at[g, k], ((gx + k) % GX, gy))
            )
        return copies

    def start(copies):
        for copy in copies:
            copy.start()

    def arrive(copies):
        for copy in copies:
            copy.wait_recv()

    def sum0(g):
        for i in range(4):
            s0[g, i] = part[g, core, i] + r0[g, i]

    def sum1(g):
        a1[g] = (s0[g, px, :, pl.ds(0, 10)] + r1a[g, 0]) + (r1a[g, 1] + r1a[g, 2])
        b1[g] = (s0[g, :, yh, pl.ds(10 + 5 * yl, 5)] + r1b[g, 0]) + (r1b[g, 1] + r1b[g, 2])
        c1[g] = (s0[g, :, :, pl.ds(20 + 2 * pz, 2)] + r1c[g, 0]) + (r1c[g, 1] + r1c[g, 2])

    def sum2(g):
        ab2[g, 0] = (a1[g, yh, pl.ds(5 * yl, 5)] + r2a[g, 0]) + (r2a[g, 1] + r2a[g, 2])
        ab2[g, 1] = (b1[g, px] + r2b[g, 0]) + (r2b[g, 1] + r2b[g, 2])
        c2[g] = (c1[g, px] + r2c[g, 0]) + (r2c[g, 1] + r2c[g, 2])

    def sum3(g):
        ab3[g] = (ab2[g] + r3[g, 0]) + (r3[g, 1] + r3[g, 2])
        c3[g] = (c2[g, yh, yl] + r3c[g, 0]) + (r3c[g, 1] + r3c[g, 2])

    def sum4(g):
        for i in range(2):
            done[g, pl.ds(10 * i + 5 * yl, 5)] = ab3[g, i] * scale
            done[g, pl.ds(10 * i + 5 * (1 - yl), 5)] = r4[g, i] * scale
        done[g, 20 + 2 * pz + yl] = c3[g] * scale
        for k in range(1, GX):
            source = (gx + GX - k) % GX
            done[g, 20 + 2 * (source % 4) + source // 4] = rc4[g, k - 1] * scale

    for g in range(2):
        part[g, :, :, :, 27] = jnp.zeros((2, 4, 2, 8, C), F32)

    for f, raw in enumerate((feat, cot)):
        loads[f].wait()
        for x in range(X):
            for b in range(2):
                rows = raw[x, pl.ds(4 * b, 4)].astype(F32) * mask[b][None, None]
                fu[f, 1, x + 1, pl.ds(4 * b + 1, 4)] = rows.astype(BF16)
    halo_zero(fu)
    halo_zero(hq)

    wide_x = 1 + (gx > 0).astype(jnp.int32) + (gx < GX - 1).astype(jnp.int32)
    wide_y = 1 + (gy > 0).astype(jnp.int32) + (gy < GY - 1).astype(jnp.int32)
    pl.semaphore_wait(barrier, len(fixed) + wide_x * wide_y - 1)

    halo_start(fu, 0)
    for f in range(2):
        shift_inner(fu.at[f])
    loads[2].wait()
    loads[3].wait()
    forward(INNER)
    backward(INNER)
    halo_wait(fu, 0)
    for f in range(2):
        shift_rim(fu.at[f])
    forward(RIM)
    halo_start(hq.at[0], 1)
    wgrad(1, hq.at[0], fu.at[1], True)
    start(stage0(1))
    backward(RIM)
    halo_start(hq.at[1], 2)
    shift_inner(hq.at[0])
    shift_inner(hq.at[1])
    arrive(stage0(1))
    sum0(1)
    start(stage1(1))
    wgrad(0, hq.at[1], fu.at[0], False)
    start(stage0(0))
    halo_wait(hq.at[0], 1)
    shift_rim(hq.at[0])
    arrive(stage1(1))
    sum1(1)
    start(stage2(1))
    arrive(stage0(0))
    sum0(0)
    start(stage1(0))
    finish(0, w2, False, ALL)
    out_copy = pltpu.make_async_copy(outs.at[0], out_hbm, out_sem.at[0])
    out_copy.start()
    halo_wait(hq.at[1], 2)
    shift_rim(hq.at[1])
    arrive(stage2(1))
    sum2(1)
    start(stage3(1))
    finish(1, w1, True, ALL)
    gf_copy = pltpu.make_async_copy(outs.at[1], gf_hbm, out_sem.at[1])
    gf_copy.start()
    arrive(stage3(1))
    sum3(1)
    start(stage4(1))
    arrive(stage1(0))
    sum1(0)
    start(stage2(0))
    arrive(stage2(0))
    sum2(0)
    start(stage3(0))
    arrive(stage4(1))
    sum4(1)
    g2_copy = pltpu.make_async_copy(done.at[1, pl.ds(0, 27)], g2_hbm, out_sem.at[2])
    g2_copy.start()
    arrive(stage3(0))
    sum3(0)
    start(stage4(0))
    arrive(stage4(0))
    sum4(0)
    g1_copy = pltpu.make_async_copy(done.at[0, pl.ds(0, 27)], g1_hbm, out_sem.at[3])
    g1_copy.start()

    halo_sent(fu, 0)
    halo_sent(hq.at[0], 1)
    halo_sent(hq.at[1], 2)
    for g in range(2):
        for stage in (stage0, stage1, stage2, stage3, stage4):
            for copy in stage(g):
                copy.wait_send()
    for copy in (out_copy, gf_copy, g2_copy, g1_copy):
        copy.wait()


def body(features, w_first, w_second, occupancy, cotangent):
    scale = 1.0 / math.sqrt(GX * GY * X * Y * Z)
    anyspace = pl.BlockSpec(memory_space=pl.ANY)
    dma = pltpu.SemaphoreType.DMA
    vm = pltpu.VMEM
    tile = (8, C)
    split = (X, 8, 2, Z, C)
    out, grad, first, second = pl.pallas_call(
        functools.partial(kernel, scale),
        name="section",
        out_shape=(
            jax.ShapeDtypeStruct((X, 8, 2, Z, C), BF16),
            jax.ShapeDtypeStruct((X, 8, 2, Z, C), BF16),
            jax.ShapeDtypeStruct((27, 8, C), F32),
            jax.ShapeDtypeStruct((27, 8, C), F32),
        ),
        in_specs=[pl.BlockSpec(memory_space=pltpu.SMEM)] + [anyspace] * 4,
        out_specs=(anyspace,) * 4,
        scratch_shapes=[
            vm((X, 8, 2, Z, C), BF16),
            vm((X, 8, 2, Z, C), BF16),
            vm((27, C, C), BF16),
            vm((27, C, C), BF16),
            vm((2, 3, X + 2, 10, 2, Z, C), BF16),
            vm((2, 3, X + 2, 10, 2, Z, C), BF16),
            vm((X, 8, Z, 2 * C), F32),
            vm((2, X, C, 8 * Z), BF16),
            vm((2, X, 8, 2, Z, C), BF16),
            vm((2, 2, 4, 2, TAPS, *tile), F32),
            vm((2, 4, 2, TAPS, *tile), F32),
            vm((2, 4, 2, TAPS, *tile), F32),
            vm((2, 3, 2, 10, *tile), F32),
            vm((2, 3, 4, 5, *tile), F32),
            vm((2, 3, 4, 2, 2, *tile), F32),
            vm((2, 2, 10, *tile), F32),
            vm((2, 4, 5, *tile), F32),
            vm((2, 4, 2, 2, *tile), F32),
            vm((2, 3, 5, *tile), F32),
            vm((2, 3, 5, *tile), F32),
            vm((2, 3, 2, 2, *tile), F32),
            vm((2, 2, 5, *tile), F32),
            vm((2, 2, 2, *tile), F32),
            vm((2, 3, 2, 5, *tile), F32),
            vm((2, 3, *tile), F32),
            vm((2, 2, 5, *tile), F32),
            vm((2, *tile), F32),
            vm((2, 2, 5, *tile), F32),
            vm((2, 7, *tile), F32),
            vm((2, TAPS, *tile), F32),
            dma((4,)),
            dma((4,)),
            dma((3, 8)),
            dma((3, 8)),
            dma((2,)),
            dma((2,)),
            dma((2, 3, 3)),
            dma((2, 3, 3)),
            dma((2, 3, 3)),
            dma((2, 3, 3)),
            dma((2, 2, 3)),
            dma((2, 2, 3)),
            dma((2, 8)),
            dma((2, 8)),
        ],
        compiler_params=pltpu.CompilerParams(
            collective_id=0, has_side_effects=True, vmem_limit_bytes=62 * 2**20
        ),
    )(occupancy, features.reshape(split), cotangent.reshape(split), w_first, w_second)
    return out.reshape(features.shape), grad.reshape(features.shape), first, second


def solution(mesh):
    in_specs = (P("gx", "gy", None, None), P(), P(), P("gx", "gy", None), P("gx", "gy", None, None))
    out_specs = (
        P("gx", "gy", None, None),
        P("gx", "gy", None, None),
        P(None, "gy", None),
        P(None, "gy", None),
    )
    return jax.shard_map(body, mesh=mesh, in_specs=in_specs, out_specs=out_specs, check_vma=False)
```

```python
import functools
import math

import jax
import jax.numpy as jnp
from jax import lax
from jax.experimental import pallas as pl
from jax.experimental.pallas import tpu as pltpu
from jax.sharding import PartitionSpec as P

F32 = jnp.float32
BF16 = jnp.bfloat16
MESH = pl.DeviceIdType.MESH
DIRS = [(ax, ay) for ax in (-1, 0, 1) for ay in (-1, 0, 1) if (ax, ay) != (0, 0)]
GX, GY = 8, 16
X, Y, Z, C = 8, 16, 16, 128
TAPS = 28
FRONT = [(0, 2, 0, 8)], [(2, 2, 0, 8)]
BACK = [(4, 2, 0, 8)], [(6, 2, 0, 8)]
INNER = [(1, 3, 1, 6)], [(4, 3, 1, 6)]
RIM = [(0, 1, 0, 8), (1, 6, 0, 1)], [(7, 1, 0, 8), (1, 6, 7, 1)]

FULL = ("x", "yh", "z", "yl")
SIZE = {"x": 4, "yh": 2, "z": 4, "yl": 2}
PARTS = (
    (0, FULL, ("x", "z", "y")),
    (8, FULL, ("y", "x", "z")),
    (16, FULL, ("z", "y", "x")),
    (24, FULL[:3], ("x", "y", "z")),
)


def without(dims, axis):
    gone = ("yh", "yl") if axis == "y" else (axis,)
    return tuple(d for d in dims if d not in gone)


def dims_after(part, stages):
    dims = part[1]
    for axis in part[2][:stages]:
        dims = without(dims, axis)
    return dims


def shape_of(dims):
    return tuple(SIZE[d] for d in dims) + (8, C)


def kernel(scale, names, *refs):
    ref = dict(zip(names, refs))
    occ_ref, feat_hbm, cot_hbm, w1_hbm, w2_hbm = (ref[n] for n in ("occ", "f_in", "c_in", "w1_in", "w2_in"))
    out_hbm, gf_hbm, g1_hbm, g2_hbm = (ref[n] for n in ("out", "gf", "g1", "g2"))
    feat, cot, w1, w2, fu, hq = (ref[n] for n in ("feat", "cot", "w1", "w2", "fu", "hq"))
    slope, at, outs, part, r0, fin, rfin, done = (
        ref[n] for n in ("slope", "at", "outs", "part", "r0", "fin", "rfin", "done")
    )
    in_sem, out_sem, hs, hr, s0s, s0r, rss, rsr, s4s, s4r = (
        ref[n] for n in ("in_sem", "out_sem", "hs", "hr", "s0s", "s0r", "rss", "rsr", "s4s", "s4r")
    )
    gx = lax.axis_index("gx")
    gy = lax.axis_index("gy")
    core = gy % 2
    px = (gy // 2) % 4
    yh = gy // 8
    pz = gx % 4
    yl = gx // 4
    py = yh * 2 + yl

    def at_x(k):
        return (px + k) % 4

    def at_y(k):
        return (py + k) % 4

    def at_z(k):
        return (pz + k) % 4

    def dev_x(k):
        return (gx, yh * 8 + at_x(k) * 2 + core)

    def dev_y(k):
        to = at_y(k)
        return ((to % 2) * 4 + pz, (to // 2) * 8 + px * 2 + core)

    def dev_z(k):
        return (yl * 4 + at_z(k), gy)

    partner = (gx, gy + 1 - 2 * core)

    def exists(ax, ay):
        ok = None
        for step, pos, size in ((ax, gx, GX), (ay, gy, GY)):
            if step == 0:
                continue
            here = pos + 1 < size if step > 0 else pos > 0
            ok = here if ok is None else jnp.logical_and(ok, here)
        return ok

    barrier = pltpu.get_barrier_semaphore()
    for ax, ay in DIRS:
        @pl.when(exists(ax, ay))
        def _():
            pl.semaphore_signal(barrier, inc=1, device_id=(gx + ax, gy + ay), device_id_type=MESH)
    fixed = [partner] + [dev_x(k) for k in (1, 2, 3)] + [dev_y(k) for k in (1, 2, 3)]
    fixed += [((gx + k) % GX, gy) for k in range(1, GX)]
    for peer in fixed:
        pl.semaphore_signal(barrier, inc=1, device_id=peer, device_id_type=MESH)

    loads = [
        pltpu.make_async_copy(src, dst, in_sem.at[i])
        for i, (src, dst) in enumerate(
            ((feat_hbm, feat), (cot_hbm, cot), (w1_hbm, w1), (w2_hbm, w2))
        )
    ]
    for load in loads:
        load.start()

    low = lax.broadcasted_iota(jnp.int32, (Z, C), 0) < 8
    mask = [
        jnp.where(low, occ_ref[0, b, 0].astype(F32), occ_ref[0, b, 1].astype(F32)) for b in range(2)
    ]

    def mask_rows(boxes, wide):
        rows = []
        for x0, nx, k0, nk in boxes:
            for _ in range(nx):
                rows += [mask[k // 4] for k in range(k0, k0 + nk)]
        m = jnp.concatenate(rows, axis=0)
        return jnp.concatenate([m, m], axis=1) if wide else m

    def z_shift(field, at_index):
        v = field[(1, *at_index)].astype(F32)
        t = v.reshape(-1, Z, C)
        z = lax.broadcasted_iota(jnp.int32, (1, Z, C), 1)
        down = jnp.where(z == 0, 0.0, pltpu.roll(t, 1, 1))
        up = jnp.where(z == Z - 1, 0.0, pltpu.roll(t, Z - 1, 1))
        field[(0, *at_index)] = down.astype(BF16).reshape(v.shape)
        field[(2, *at_index)] = up.astype(BF16).reshape(v.shape)

    def edge_x(step, recv):
        if step == 0:
            return (pl.ds(1, X),)
        if recv:
            return (0 if step > 0 else X + 1,)
        return (X if step > 0 else 1,)

    def edge_y(step, recv):
        if step == 0:
            return (pl.ds(1, 8),)
        if recv:
            return (0, 1) if step > 0 else (9, 0)
        return (8, 1) if step > 0 else (1, 0)

    def halo_copy(ref, d, slot):
        ax, ay = DIRS[d]
        return pltpu.make_async_remote_copy(
            src_ref=ref.at[(1, *edge_x(ax, False), *edge_y(ay, False))],
            dst_ref=ref.at[(1, *edge_x(ax, True), *edge_y(ay, True))],
            send_sem=hs.at[slot, d],
            recv_sem=hr.at[slot, d],
            device_id=(gx + ax, gy + ay),
            device_id_type=MESH,
        )

    def halo_start(ref, slot):
        for d, (ax, ay) in enumerate(DIRS):
            @pl.when(exists(ax, ay))
            def _():
                halo_copy(ref, d, slot).start()

    def halo_zero(ref):
        for ax, ay in DIRS:
            @pl.when(jnp.logical_not(exists(-ax, -ay)))
            def _():
                index = (1, *edge_x(ax, True), *edge_y(ay, True))
                ref[index] = jnp.zeros(ref.at[index].shape, BF16)

    def halo_wait(ref, slot):
        for d, (ax, ay) in enumerate(DIRS):
            @pl.when(exists(-ax, -ay))
            def _():
                halo_copy(ref, d, slot).wait_recv()

    def halo_sent(ref, slot):
        for d, (ax, ay) in enumerate(DIRS):
            @pl.when(exists(ax, ay))
            def _():
                halo_copy(ref, d, slot).wait_send()

    def shift_rim(field):
        for x in (0, X + 1):
            z_shift(field, (x,))
        for edge in ((0, 1), (9, 0)):
            z_shift(field, (pl.ds(1, X), *edge))

    def shift_inner(field):
        for x in range(1, X + 1):
            z_shift(field, (x, pl.ds(1, 8)))

    def rows_of(field, boxes, dz, dx, j):
        halves = []
        for h in range(2):
            pieces = [
                field[dz, pl.ds(x0 + dx, nx), pl.ds(k0 + j + h, nk), 1 - h].reshape(nx * nk * Z, C)
                for x0, nx, k0, nk in boxes
            ]
            halves.append(jnp.concatenate(pieces, axis=0) if len(pieces) > 1 else pieces[0])
        return jnp.concatenate(halves, axis=1)

    zero = jnp.zeros((C, C), BF16)

    def conv(field, w, boxes, flipped):
        left, right = [], []
        for dx in range(3):
            for dz in range(3):
                tap = [w[26 - (9 * dx + 3 * dy + dz)] if flipped else w[9 * dx + 3 * dy + dz] for dy in range(3)]
                for j in range(2):
                    left.append(rows_of(field, boxes, dz, dx, j))
                    if j == 0:
                        grid = ((tap[0], zero), (tap[1], tap[0]))
                    else:
                        grid = ((tap[2], tap[1]), (zero, tap[2]))
                    if flipped:
                        grid = tuple(zip(*grid))
                        right.append(jnp.concatenate([jnp.concatenate(r, axis=1) for r in grid], axis=0))
                    else:
                        right.append(jnp.concatenate([jnp.concatenate(r, axis=1) for r in grid], axis=0))
        lhs = jnp.concatenate(left, axis=1)
        if flipped:
            return lax.dot_general(
                lhs, jnp.concatenate(right, axis=1), (((1,), (1,)), ((), ())), preferred_element_type=F32
            )
        return jnp.dot(lhs, jnp.concatenate(right, axis=0), preferred_element_type=F32)

    def tiles(boxes):
        at_row = 0
        for x0, nx, k0, nk in boxes:
            n = nx * nk * Z
            yield (x0, nx, k0, nk), slice(at_row, at_row + n)
            at_row += n

    def put(field_at, boxes, value):
        for (x0, nx, k0, nk), rows in tiles(boxes):
            for h in range(2):
                field_at(x0, nx, k0, nk, h, value[rows, h * C : (h + 1) * C].reshape(nx, nk, Z, C))

    def put_padded(field):
        def store(x0, nx, k0, nk, h, v):
            field[1, pl.ds(x0 + 1, nx), pl.ds(k0 + 1, nk), h] = v.astype(BF16)
        return store

    def forward(pair):
        pres = [conv(fu.at[0], w1, boxes, False) for boxes in pair]
        for pre, boxes in zip(pres, pair):
            s = jax.nn.sigmoid(pre)
            m = mask_rows(boxes, True)
            put(put_padded(hq.at[0]), boxes, m * (pre * s))
            d = m * (s * (1.0 + pre * (1.0 - s)))
            for (x0, nx, k0, nk), rows in tiles(boxes):
                slope[pl.ds(x0, nx), pl.ds(k0, nk)] = d[rows].reshape(nx, nk, Z, 2 * C)

    def backward(pair):
        grads = [conv(fu.at[1], w2, boxes, True) for boxes in pair]
        for grad, boxes in zip(grads, pair):
            d = [slope[pl.ds(x0, nx), pl.ds(k0, nk)].reshape(nx * nk * Z, 2 * C) for x0, nx, k0, nk in boxes]
            d = jnp.concatenate(d, axis=0) if len(d) > 1 else d[0]
            put(put_padded(hq.at[1]), boxes, grad * d)

    def finish(slot, w, flipped, pair):
        accs = [conv(hq.at[slot], w, boxes, flipped) for boxes in pair]
        base = fu.at[slot]

        def store(x0, nx, k0, nk, h, v):
            b = base[1, pl.ds(x0 + 1, nx), pl.ds(k0 + 1, nk), h].astype(F32)
            outs[slot, pl.ds(x0, nx), pl.ds(k0, nk), h] = (b + v).astype(BF16)
        for acc, boxes in zip(accs, pair):
            put(store, boxes, acc * mask_rows(boxes, True))

    def turn(left):
        for h in range(2):
            for x in range(X):
                at[h, x] = left[1, x + 1, pl.ds(1, 8), h].reshape(8 * Z, C).T

    def wgrad(g, p, right, mirrored):
        lhs = jnp.concatenate([at[h, x] for h in range(2) for x in range(X)], axis=1)
        first = PARTS[p][0]
        middle = first + 4 if p < 3 else first + 2
        pair = range(first, middle), range(middle, min(first + 8, 27))
        sums = []
        for taps in pair:
            cols = []
            for tap in taps:
                dx, dy, dz = tap // 9, tap // 3 % 3, tap % 3
                ex, ey, ez = (2 - dx, 2 - dy, 2 - dz) if mirrored else (dx, dy, dz)
                halves = []
                for h in range(2):
                    row = h + ey + 1
                    halves.append(right[ez, pl.ds(ex, X), pl.ds(row // 2, 8), row % 2].reshape(X * 8 * Z, C))
                cols.append(jnp.concatenate(halves, axis=0))
            rhs = jnp.concatenate(cols, axis=1) if len(cols) > 1 else cols[0]
            sums.append(jnp.dot(lhs, rhs, preferred_element_type=F32))
        for acc, taps in zip(sums, pair):
            for i, tap in enumerate(taps):
                block = acc[:, i * C : (i + 1) * C]
                if not mirrored:
                    block = block.T
                for s in range(16):
                    part[g, s % 2, (s // 2) % 4, s // 8, tap] = block[8 * s : 8 * s + 8]
        start(stage0(g, p))

    def remote(src, dst, send, recv, to):
        return pltpu.make_async_remote_copy(
            src_ref=src, dst_ref=dst, send_sem=send, recv_sem=recv, device_id=to, device_id_type=MESH
        )

    def count(p):
        return 8 if p < 3 else 4

    def stage0(g, p):
        taps = pl.ds(PARTS[p][0], count(p))
        return [
            remote(
                part.at[g, 1 - core, :, :, taps], r0.at[g, :, :, taps], s0s.at[g, p], s0r.at[g, p], partner
            )
        ]

    def pick(dims, axis, pos):
        index = []
        for d in dims:
            if d == axis:
                index.append(pos)
            elif axis == "y" and d == "yh":
                index.append(pos // 2)
            elif axis == "y" and d == "yl":
                index.append(pos % 2)
            else:
                index.append(slice(None))
        return tuple(index)

    position = {"x": (at_x, dev_x), "y": (at_y, dev_y), "z": (at_z, dev_z)}

    def ring(g, p, stage):
        dims = dims_after(PARTS[p], stage - 1)
        axis = PARTS[p][2][stage - 1]
        where, device = position[axis]
        source = ref[f"h{p}"] if stage == 1 else ref[f"t{p}_{stage - 1}"]
        return [
            remote(
                source.at[(g, *pick(dims, axis, where(k)))],
                ref[f"r{p}_{stage}"].at[g, k - 1],
                rss.at[g, p, stage - 1, k - 1],
                rsr.at[g, p, stage - 1, k - 1],
                device(k),
            )
            for k in (1, 2, 3)
        ]

    def gather(g):
        return [
            remote(fin.at[g], rfin.at[g, k - 1], s4s.at[g, k - 1], s4r.at[g, k - 1], ((gx + k) % GX, gy))
            for k in range(1, GX)
        ]

    def start(copies):
        for copy in copies:
            copy.start()

    def arrive(copies):
        for copy in copies:
            copy.wait_recv()

    def step0(g, p):
        arrive(stage0(g, p))
        first = PARTS[p][0]
        for i in range(count(p)):
            total = part[g, core, :, :, first + i] + r0[g, :, :, first + i]
            index = (g, slice(None), slice(None)) + ((i // 2, i % 2) if p < 3 else (i,))
            ref[f"t{p}_0"][index] = total
            ref[f"h{p}"][index] = total.astype(BF16)
        start(ring(g, p, 1))

    def step(g, p, stage):
        arrive(ring(g, p, stage))
        dims = dims_after(PARTS[p], stage - 1)
        axis = PARTS[p][2][stage - 1]
        own = ref[f"t{p}_{stage - 1}"][(g, *pick(dims, axis, position[axis][0](0)))]
        r = ref[f"r{p}_{stage}"]
        total = (own + r[g, 0].astype(F32)) + (r[g, 1].astype(F32) + r[g, 2].astype(F32))
        if stage < 3:
            ref[f"t{p}_{stage}"][g] = total
            start(ring(g, p, stage + 1))
        else:
            fin[g, p] = total

    def spread(g):
        start(gather(g))

    def collect(g, target, sem):
        for p in range(3):
            done[g, 8 * p + 2 * pz + yl] = fin[g, p] * scale

        @pl.when(yl == 0)
        def _():
            done[g, 24 + pz] = fin[g, 3] * scale
        for k, copy in enumerate(gather(g), 1):
            copy.wait_recv()
            source = (gx + GX - k) % GX
            for p in range(3):
                done[g, 8 * p + 2 * (source % 4) + source // 4] = rfin[g, k - 1, p] * scale

            @pl.when(source < 4)
            def _():
                done[g, 24 + source] = rfin[g, k - 1, 3] * scale
        copy = pltpu.make_async_copy(done.at[g, pl.ds(0, 27)], target, out_sem.at[sem])
        copy.start()
        return copy

    for g in range(2):
        part[g, :, :, :, 27] = jnp.zeros((2, 4, 2, 8, C), F32)

    for f, raw in enumerate((feat, cot)):
        loads[f].wait()
        for x in range(X):
            for b in range(2):
                rows = raw[x, pl.ds(4 * b, 4)].astype(F32) * mask[b][None, None]
                fu[f, 1, x + 1, pl.ds(4 * b + 1, 4)] = rows.astype(BF16)
    for f in range(2):
        halo_zero(fu.at[f])
        halo_zero(hq.at[f])

    wide_x = 1 + (gx > 0).astype(jnp.int32) + (gx < GX - 1).astype(jnp.int32)
    wide_y = 1 + (gy > 0).astype(jnp.int32) + (gy < GY - 1).astype(jnp.int32)
    pl.semaphore_wait(barrier, len(fixed) + wide_x * wide_y - 1)

    halo_start(fu.at[0], 0)
    halo_start(fu.at[1], 1)
    for f in range(2):
        shift_inner(fu.at[f])
    loads[2].wait()
    loads[3].wait()
    forward(INNER)
    backward(INNER)
    halo_wait(fu.at[0], 0)
    shift_rim(fu.at[0])
    forward(RIM)
    halo_start(hq.at[0], 2)
    halo_wait(fu.at[1], 1)
    shift_rim(fu.at[1])
    turn(hq.at[0])
    wgrad(1, 0, fu.at[1], True)
    wgrad(1, 1, fu.at[1], True)
    wgrad(1, 2, fu.at[1], True)
    step0(1, 0)
    wgrad(1, 3, fu.at[1], True)
    step0(1, 1)
    backward(RIM)
    halo_start(hq.at[1], 3)
    step0(1, 2)
    step0(1, 3)
    turn(hq.at[1])
    wgrad(0, 0, fu.at[0], False)
    wgrad(0, 1, fu.at[0], False)
    wgrad(0, 2, fu.at[0], False)
    step0(0, 0)
    wgrad(0, 3, fu.at[0], False)
    step0(0, 1)
    shift_inner(hq.at[0])
    halo_wait(hq.at[0], 2)
    shift_rim(hq.at[0])
    step0(0, 2)
    step(1, 0, 1)
    step(1, 1, 1)
    step0(0, 3)
    step(1, 2, 1)
    step(1, 3, 1)
    finish(0, w2, False, FRONT)
    step(1, 0, 2)
    step(1, 1, 2)
    step(1, 2, 2)
    step(1, 3, 2)
    finish(0, w2, False, BACK)
    out_copy = pltpu.make_async_copy(outs.at[0], out_hbm, out_sem.at[0])
    out_copy.start()
    step(0, 0, 1)
    step(0, 1, 1)
    shift_inner(hq.at[1])
    halo_wait(hq.at[1], 3)
    shift_rim(hq.at[1])
    step(0, 2, 1)
    step(0, 3, 1)
    finish(1, w1, True, FRONT)
    step(1, 0, 3)
    step(1, 1, 3)
    step(1, 2, 3)
    step(1, 3, 3)
    spread(1)
    step(0, 0, 2)
    step(0, 1, 2)
    step(0, 2, 2)
    step(0, 3, 2)
    finish(1, w1, True, BACK)
    gf_copy = pltpu.make_async_copy(outs.at[1], gf_hbm, out_sem.at[1])
    gf_copy.start()
    step(0, 0, 3)
    step(0, 1, 3)
    step(0, 2, 3)
    step(0, 3, 3)
    spread(0)
    g2_copy = collect(1, g2_hbm, 2)
    g1_copy = collect(0, g1_hbm, 3)

    for slot, field in enumerate((fu.at[0], fu.at[1], hq.at[0], hq.at[1])):
        halo_sent(field, slot)
    for g in range(2):
        sent = gather(g)
        for p in range(4):
            sent += stage0(g, p) + ring(g, p, 1) + ring(g, p, 2) + ring(g, p, 3)
        for copy in sent:
            copy.wait_send()
    for copy in (out_copy, gf_copy, g2_copy, g1_copy):
        copy.wait()


def hand_on(a, b, c, d, a_out, b_out, c_out, d_out):
    for source, target in ((a, a_out), (b, b_out), (c, c_out), (d, d_out)):
        target[...] = source[...]


def body(features, w_first, w_second, occupancy, cotangent):
    scale = 1.0 / math.sqrt(GX * GY * X * Y * Z)
    anyspace = pl.BlockSpec(memory_space=pl.ANY)
    dma = pltpu.SemaphoreType.DMA
    vm = pltpu.VMEM
    split = (X, 8, 2, Z, C)
    field = (2, 3, X + 2, 10, 2, Z, C)
    tile = (8, C)
    scratch = {
        "feat": vm(split, BF16),
        "cot": vm(split, BF16),
        "w1": vm((27, C, C), BF16),
        "w2": vm((27, C, C), BF16),
        "fu": vm(field, BF16),
        "hq": vm(field, BF16),
        "slope": vm((X, 8, Z, 2 * C), F32),
        "at": vm((2, X, C, 8 * Z), BF16),
        "outs": vm((2, *split), BF16),
        "part": vm((2, 2, 4, 2, TAPS, *tile), F32),
        "r0": vm((2, 4, 2, TAPS, *tile), F32),
        "fin": vm((2, 4, *tile), F32),
        "rfin": vm((2, 7, 4, *tile), F32),
        "done": vm((2, TAPS, *tile), F32),
        "in_sem": dma((4,)),
        "out_sem": dma((4,)),
        "hs": dma((4, 8)),
        "hr": dma((4, 8)),
        "s0s": dma((2, 4)),
        "s0r": dma((2, 4)),
        "rss": dma((2, 4, 3, 3)),
        "rsr": dma((2, 4, 3, 3)),
        "s4s": dma((2, 7)),
        "s4r": dma((2, 7)),
    }
    for p, part in enumerate(PARTS):
        scratch[f"h{p}"] = vm((2, *shape_of(part[1])), BF16)
        for stage in range(4):
            shape = shape_of(dims_after(part, stage))
            if stage < 3:
                scratch[f"t{p}_{stage}"] = vm((2, *shape), F32)
            if stage > 0:
                scratch[f"r{p}_{stage}"] = vm((2, 3, *shape), BF16 if stage == 1 else F32)
    names = ("occ", "f_in", "c_in", "w1_in", "w2_in", "out", "gf", "g1", "g2", *scratch)
    shapes = (
        jax.ShapeDtypeStruct(split, BF16),
        jax.ShapeDtypeStruct(split, BF16),
        jax.ShapeDtypeStruct((27, 8, C), F32),
        jax.ShapeDtypeStruct((27, 8, C), F32),
    )
    stay = [
        pltpu.with_memory_space_constraint(a, pltpu.HBM)
        for a in (features.reshape(split), cotangent.reshape(split), w_first, w_second)
    ]
    results = pl.pallas_call(
        functools.partial(kernel, scale, names),
        name="section",
        out_shape=shapes,
        in_specs=[pl.BlockSpec(memory_space=pltpu.SMEM)] + [pl.BlockSpec(memory_space=pltpu.HBM)] * 4,
        out_specs=(anyspace,) * 4,
        scratch_shapes=list(scratch.values()),
        compiler_params=pltpu.CompilerParams(
            collective_id=0, has_side_effects=True, vmem_limit_bytes=48 * 2**20
        ),
    )(occupancy, *stay)
    local = pl.BlockSpec(memory_space=pltpu.VMEM)
    out, grad, first, second = pl.pallas_call(
        hand_on,
        name="hand_on",
        out_shape=shapes,
        in_specs=[local] * 4,
        out_specs=(local,) * 4,
        compiler_params=pltpu.CompilerParams(vmem_limit_bytes=8 * 2**20),
    )(*results)
    return out.reshape(features.shape), grad.reshape(features.shape), first, second


def solution(mesh):
    in_specs = (P("gx", "gy", None, None), P(), P(), P("gx", "gy", None), P("gx", "gy", None, None))
    out_specs = (
        P("gx", "gy", None, None),
        P("gx", "gy", None, None),
        P(None, "gy", None),
        P(None, "gy", None),
    )
    return jax.shard_map(body, mesh=mesh, in_specs=in_specs, out_specs=out_specs, check_vma=False)
```

```python
import functools
import math

import jax
import jax.numpy as jnp
from jax import lax
from jax.experimental import pallas as pl
from jax.experimental.pallas import tpu as pltpu
from jax.sharding import PartitionSpec as P

F32 = jnp.float32
BF16 = jnp.bfloat16
MESH = pl.DeviceIdType.MESH
DIRS = [(ax, ay) for ax in (-1, 0, 1) for ay in (-1, 0, 1) if (ax, ay) != (0, 0)]
GX, GY = 8, 16
X, Y, Z, C = 8, 16, 16, 128
TAPS = 28
FRONT = [(0, 2, 0, 8)], [(2, 2, 0, 8)]
BACK = [(4, 2, 0, 8)], [(6, 2, 0, 8)]
INNER = [(1, 3, 1, 6)], [(4, 3, 1, 6)]
RIM = [(0, 1, 0, 8), (1, 6, 0, 1)], [(7, 1, 0, 8), (1, 6, 7, 1)]

FULL = ("x", "yh", "z", "yl")
SIZE = {"x": 4, "yh": 2, "z": 4, "yl": 2}
PARTS = (
    (0, FULL, ("x", "z", "y")),
    (8, FULL, ("y", "x", "z")),
    (16, FULL, ("z", "y", "x")),
    (24, FULL[:3], ("x", "y", "z")),
)


def without(dims, axis):
    gone = ("yh", "yl") if axis == "y" else (axis,)
    return tuple(d for d in dims if d not in gone)


def dims_after(part, stages):
    dims = part[1]
    for axis in part[2][:stages]:
        dims = without(dims, axis)
    return dims


def shape_of(dims):
    return tuple(SIZE[d] for d in dims) + (8, C)


def kernel(scale, names, *refs):
    ref = dict(zip(names, refs))
    occ_hbm, feat_hbm, cot_hbm, w1_hbm, w2_hbm = (ref[n] for n in ("occ", "f_in", "c_in", "w1_in", "w2_in"))
    out_hbm, gf_hbm, g1_hbm, g2_hbm = (ref[n] for n in ("out", "gf", "g1", "g2"))
    feat, cot, w1, w2, fu, hq = (ref[n] for n in ("feat", "cot", "w1", "w2", "fu", "hq"))
    slope, at, outs, part, r0, fin, rfin, done = (
        ref[n] for n in ("slope", "at", "outs", "part", "r0", "fin", "rfin", "done")
    )
    occ_ref, occ_sem = ref["occ_here"], ref["occ_sem"]
    in_sem, out_sem, hs, hr, s0s, s0r, rss, rsr, s4s, s4r = (
        ref[n] for n in ("in_sem", "out_sem", "hs", "hr", "s0s", "s0r", "rss", "rsr", "s4s", "s4r")
    )
    gx = lax.axis_index("gx")
    gy = lax.axis_index("gy")
    core = gy % 2
    px = (gy // 2) % 4
    yh = gy // 8
    pz = gx % 4
    yl = gx // 4
    py = yh * 2 + yl

    def at_x(k):
        return (px + k) % 4

    def at_y(k):
        return (py + k) % 4

    def at_z(k):
        return (pz + k) % 4

    def dev_x(k):
        return (gx, yh * 8 + at_x(k) * 2 + core)

    def dev_y(k):
        to = at_y(k)
        return ((to % 2) * 4 + pz, (to // 2) * 8 + px * 2 + core)

    def dev_z(k):
        return (yl * 4 + at_z(k), gy)

    partner = (gx, gy + 1 - 2 * core)

    def exists(ax, ay):
        ok = None
        for step, pos, size in ((ax, gx, GX), (ay, gy, GY)):
            if step == 0:
                continue
            here = pos + 1 < size if step > 0 else pos > 0
            ok = here if ok is None else jnp.logical_and(ok, here)
        return ok

    get_occ = pltpu.make_async_copy(occ_hbm, occ_ref, occ_sem.at[0])
    get_occ.start()
    loads = [
        [
            pltpu.make_async_copy(src.at[pl.ds(2 * i, 2)], dst.at[pl.ds(2 * i, 2)], in_sem.at[f, i])
            for i in range(4)
        ]
        for f, (src, dst) in enumerate(((feat_hbm, feat), (cot_hbm, cot)))
    ]
    loads += [
        [pltpu.make_async_copy(src, dst, in_sem.at[f, 0])] for f, src, dst in ((2, w1_hbm, w1), (3, w2_hbm, w2))
    ]
    for group in loads:
        for load in group:
            load.start()
    barrier = pltpu.get_barrier_semaphore()
    for ax, ay in DIRS:
        @pl.when(exists(ax, ay))
        def _():
            pl.semaphore_signal(barrier, inc=1, device_id=(gx + ax, gy + ay), device_id_type=MESH)
    fixed = [partner] + [dev_x(k) for k in (1, 2, 3)] + [dev_y(k) for k in (1, 2, 3)]
    fixed += [((gx + k) % GX, gy) for k in range(1, GX)]
    for peer in fixed:
        pl.semaphore_signal(barrier, inc=1, device_id=peer, device_id_type=MESH)

    get_occ.wait()
    low = lax.broadcasted_iota(jnp.int32, (Z, C), 0) < 8
    mask = [
        jnp.where(low, occ_ref[0, b, 0].astype(F32), occ_ref[0, b, 1].astype(F32)) for b in range(2)
    ]

    def mask_rows(boxes, wide):
        rows = []
        for x0, nx, k0, nk in boxes:
            for _ in range(nx):
                rows += [mask[k // 4] for k in range(k0, k0 + nk)]
        m = jnp.concatenate(rows, axis=0)
        return jnp.concatenate([m, m], axis=1) if wide else m

    def z_shift(field, at_index):
        v = field[(1, *at_index)].astype(F32)
        t = v.reshape(-1, Z, C)
        z = lax.broadcasted_iota(jnp.int32, (1, Z, C), 1)
        down = jnp.where(z == 0, 0.0, pltpu.roll(t, 1, 1))
        up = jnp.where(z == Z - 1, 0.0, pltpu.roll(t, Z - 1, 1))
        field[(0, *at_index)] = down.astype(BF16).reshape(v.shape)
        field[(2, *at_index)] = up.astype(BF16).reshape(v.shape)

    def edge_x(step, recv):
        if step == 0:
            return (pl.ds(1, X),)
        if recv:
            return (0 if step > 0 else X + 1,)
        return (X if step > 0 else 1,)

    def edge_y(step, recv):
        if step == 0:
            return (pl.ds(1, 8),)
        if recv:
            return (0, 1) if step > 0 else (9, 0)
        return (8, 1) if step > 0 else (1, 0)

    def halo_copy(ref, d, slot):
        ax, ay = DIRS[d]
        return pltpu.make_async_remote_copy(
            src_ref=ref.at[(1, *edge_x(ax, False), *edge_y(ay, False))],
            dst_ref=ref.at[(1, *edge_x(ax, True), *edge_y(ay, True))],
            send_sem=hs.at[slot, d],
            recv_sem=hr.at[slot, d],
            device_id=(gx + ax, gy + ay),
            device_id_type=MESH,
        )

    def halo_start(ref, slot):
        for d, (ax, ay) in enumerate(DIRS):
            @pl.when(exists(ax, ay))
            def _():
                halo_copy(ref, d, slot).start()

    def halo_zero(ref):
        for ax, ay in DIRS:
            @pl.when(jnp.logical_not(exists(-ax, -ay)))
            def _():
                index = (1, *edge_x(ax, True), *edge_y(ay, True))
                ref[index] = jnp.zeros(ref.at[index].shape, BF16)

    def halo_wait(ref, slot):
        for d, (ax, ay) in enumerate(DIRS):
            @pl.when(exists(-ax, -ay))
            def _():
                halo_copy(ref, d, slot).wait_recv()

    def halo_sent(ref, slot):
        for d, (ax, ay) in enumerate(DIRS):
            @pl.when(exists(ax, ay))
            def _():
                halo_copy(ref, d, slot).wait_send()

    def shift_rim(field):
        for x in (0, X + 1):
            z_shift(field, (x,))
        for edge in ((0, 1), (9, 0)):
            z_shift(field, (pl.ds(1, X), *edge))

    def shift_inner(field):
        for x in range(1, X + 1):
            z_shift(field, (x, pl.ds(1, 8)))

    def rows_of(field, boxes, dz, dx, j):
        halves = []
        for h in range(2):
            pieces = [
                field[dz, pl.ds(x0 + dx, nx), pl.ds(k0 + j + h, nk), 1 - h].reshape(nx * nk * Z, C)
                for x0, nx, k0, nk in boxes
            ]
            halves.append(jnp.concatenate(pieces, axis=0) if len(pieces) > 1 else pieces[0])
        return jnp.concatenate(halves, axis=1)

    zero = jnp.zeros((C, C), BF16)

    def conv(field, w, boxes, flipped):
        left, right = [], []
        for dx in range(3):
            for dz in range(3):
                tap = [w[26 - (9 * dx + 3 * dy + dz)] if flipped else w[9 * dx + 3 * dy + dz] for dy in range(3)]
                for j in range(2):
                    left.append(rows_of(field, boxes, dz, dx, j))
                    if j == 0:
                        grid = ((tap[0], zero), (tap[1], tap[0]))
                    else:
                        grid = ((tap[2], tap[1]), (zero, tap[2]))
                    if flipped:
                        grid = tuple(zip(*grid))
                        right.append(jnp.concatenate([jnp.concatenate(r, axis=1) for r in grid], axis=0))
                    else:
                        right.append(jnp.concatenate([jnp.concatenate(r, axis=1) for r in grid], axis=0))
        lhs = jnp.concatenate(left, axis=1)
        if flipped:
            return lax.dot_general(
                lhs, jnp.concatenate(right, axis=1), (((1,), (1,)), ((), ())), preferred_element_type=F32
            )
        return jnp.dot(lhs, jnp.concatenate(right, axis=0), preferred_element_type=F32)

    def tiles(boxes):
        at_row = 0
        for x0, nx, k0, nk in boxes:
            n = nx * nk * Z
            yield (x0, nx, k0, nk), slice(at_row, at_row + n)
            at_row += n

    def put(field_at, boxes, value):
        for (x0, nx, k0, nk), rows in tiles(boxes):
            for h in range(2):
                field_at(x0, nx, k0, nk, h, value[rows, h * C : (h + 1) * C].reshape(nx, nk, Z, C))

    def put_padded(field):
        def store(x0, nx, k0, nk, h, v):
            field[1, pl.ds(x0 + 1, nx), pl.ds(k0 + 1, nk), h] = v.astype(BF16)
        return store

    def forward(pair):
        pres = [conv(fu.at[0], w1, boxes, False) for boxes in pair]
        for pre, boxes in zip(pres, pair):
            s = jax.nn.sigmoid(pre)
            m = mask_rows(boxes, True)
            put(put_padded(hq.at[0]), boxes, m * (pre * s))
            d = m * (s * (1.0 + pre * (1.0 - s)))
            for (x0, nx, k0, nk), rows in tiles(boxes):
                slope[pl.ds(x0, nx), pl.ds(k0, nk)] = d[rows].reshape(nx, nk, Z, 2 * C)

    def backward(pair):
        grads = [conv(fu.at[1], w2, boxes, True) for boxes in pair]
        for grad, boxes in zip(grads, pair):
            d = [slope[pl.ds(x0, nx), pl.ds(k0, nk)].reshape(nx * nk * Z, 2 * C) for x0, nx, k0, nk in boxes]
            d = jnp.concatenate(d, axis=0) if len(d) > 1 else d[0]
            put(put_padded(hq.at[1]), boxes, grad * d)

    def finish(slot, w, flipped, pair):
        accs = [conv(hq.at[slot], w, boxes, flipped) for boxes in pair]
        base = fu.at[slot]

        def store(x0, nx, k0, nk, h, v):
            b = base[1, pl.ds(x0 + 1, nx), pl.ds(k0 + 1, nk), h].astype(F32)
            outs[slot, pl.ds(x0, nx), pl.ds(k0, nk), h] = (b + v).astype(BF16)
        for acc, boxes in zip(accs, pair):
            put(store, boxes, acc * mask_rows(boxes, True))

    def turn(left):
        for h in range(2):
            for x in range(X):
                at[h, x] = left[1, x + 1, pl.ds(1, 8), h].reshape(8 * Z, C).T

    def wgrad(g, p, right, mirrored):
        lhs = jnp.concatenate([at[h, x] for h in range(2) for x in range(X)], axis=1)
        first = PARTS[p][0]
        middle = first + 4 if p < 3 else first + 2
        pair = range(first, middle), range(middle, min(first + 8, 27))
        sums = []
        for taps in pair:
            cols = []
            for tap in taps:
                dx, dy, dz = tap // 9, tap // 3 % 3, tap % 3
                ex, ey, ez = (2 - dx, 2 - dy, 2 - dz) if mirrored else (dx, dy, dz)
                halves = []
                for h in range(2):
                    row = h + ey + 1
                    halves.append(right[ez, pl.ds(ex, X), pl.ds(row // 2, 8), row % 2].reshape(X * 8 * Z, C))
                cols.append(jnp.concatenate(halves, axis=0))
            rhs = jnp.concatenate(cols, axis=1) if len(cols) > 1 else cols[0]
            sums.append(jnp.dot(lhs, rhs, preferred_element_type=F32))
        for acc, taps in zip(sums, pair):
            for i, tap in enumerate(taps):
                block = acc[:, i * C : (i + 1) * C]
                if not mirrored:
                    block = block.T
                for s in range(16):
                    part[g, s % 2, (s // 2) % 4, s // 8, tap] = block[8 * s : 8 * s + 8]
        start(stage0(g, p))

    def remote(src, dst, send, recv, to):
        return pltpu.make_async_remote_copy(
            src_ref=src, dst_ref=dst, send_sem=send, recv_sem=recv, device_id=to, device_id_type=MESH
        )

    def count(p):
        return 8 if p < 3 else 4

    def stage0(g, p):
        taps = pl.ds(PARTS[p][0], count(p))
        return [
            remote(
                part.at[g, 1 - core, :, :, taps], r0.at[g, :, :, taps], s0s.at[g, p], s0r.at[g, p], partner
            )
        ]

    def pick(dims, axis, pos):
        index = []
        for d in dims:
            if d == axis:
                index.append(pos)
            elif axis == "y" and d == "yh":
                index.append(pos // 2)
            elif axis == "y" and d == "yl":
                index.append(pos % 2)
            else:
                index.append(slice(None))
        return tuple(index)

    position = {"x": (at_x, dev_x), "y": (at_y, dev_y), "z": (at_z, dev_z)}

    def ring(g, p, stage):
        dims = dims_after(PARTS[p], stage - 1)
        axis = PARTS[p][2][stage - 1]
        where, device = position[axis]
        source = ref[f"h{p}"] if stage == 1 else ref[f"t{p}_{stage - 1}"]
        return [
            remote(
                source.at[(g, *pick(dims, axis, where(k)))],
                ref[f"r{p}_{stage}"].at[g, k - 1],
                rss.at[g, p, stage - 1],
                rsr.at[g, p, stage - 1],
                device(k),
            )
            for k in (1, 2, 3)
        ]

    def three(g, p, stage):
        every = ref[f"r{p}_{stage}"].at[g]
        return remote(every, every, rss.at[g, p, stage - 1], rsr.at[g, p, stage - 1], partner)

    def gather(g):
        return [
            remote(fin.at[g], rfin.at[g, k - 1], s4s.at[g], s4r.at[g], ((gx + k) % GX, gy))
            for k in range(1, GX)
        ]

    def seven(g):
        return remote(rfin.at[g], rfin.at[g], s4s.at[g], s4r.at[g], partner)

    def start(copies):
        for copy in copies:
            copy.start()

    def arrive(copies):
        for copy in copies:
            copy.wait_recv()

    def step0(g, p):
        arrive(stage0(g, p))
        first = PARTS[p][0]
        for i in range(count(p)):
            total = part[g, core, :, :, first + i] + r0[g, :, :, first + i]
            index = (g, slice(None), slice(None)) + ((i // 2, i % 2) if p < 3 else (i,))
            ref[f"t{p}_0"][index] = total
            ref[f"h{p}"][index] = total.astype(BF16)
        start(ring(g, p, 1))

    def step(g, p, stage):
        three(g, p, stage).wait_recv()
        dims = dims_after(PARTS[p], stage - 1)
        axis = PARTS[p][2][stage - 1]
        own = ref[f"t{p}_{stage - 1}"][(g, *pick(dims, axis, position[axis][0](0)))]
        r = ref[f"r{p}_{stage}"]
        total = (own + r[g, 0].astype(F32)) + (r[g, 1].astype(F32) + r[g, 2].astype(F32))
        if stage < 3:
            ref[f"t{p}_{stage}"][g] = total
            start(ring(g, p, stage + 1))
        else:
            fin[g, p] = total

    def settle(g):
        for p in range(4):
            stage0(g, p)[0].wait_send()
            three(g, p, 1).wait_send()
            three(g, p, 2).wait_send()
            if g == 0:
                three(1, p, 3).wait_send()
                three(0, p, 3).wait_send()

    def spread(g):
        start(gather(g))

    def collect(g, target, sem):
        for p in range(3):
            done[g, 8 * p + 2 * pz + yl] = fin[g, p] * scale

        @pl.when(yl == 0)
        def _():
            done[g, 24 + pz] = fin[g, 3] * scale
        seven(g).wait_recv()
        for k in range(1, GX):
            source = (gx + GX - k) % GX
            for p in range(3):
                done[g, 8 * p + 2 * (source % 4) + source // 4] = rfin[g, k - 1, p] * scale

            @pl.when(source < 4)
            def _():
                done[g, 24 + source] = rfin[g, k - 1, 3] * scale
        copy = pltpu.make_async_copy(done.at[g, pl.ds(0, 27)], target, out_sem.at[sem])
        copy.start()
        return copy

    for f, raw in enumerate((feat, cot)):
        for x in range(X):
            if x % 2 == 0:
                loads[f][x // 2].wait()
            for b in range(2):
                rows = raw[x, pl.ds(4 * b, 4)].astype(F32) * mask[b][None, None]
                fu[f, 1, x + 1, pl.ds(4 * b + 1, 4)] = rows.astype(BF16)
    wide_x = 1 + (gx > 0).astype(jnp.int32) + (gx < GX - 1).astype(jnp.int32)
    wide_y = 1 + (gy > 0).astype(jnp.int32) + (gy < GY - 1).astype(jnp.int32)
    pl.semaphore_wait(barrier, len(fixed) + wide_x * wide_y - 1)

    halo_start(fu.at[0], 0)
    shift_inner(fu.at[0])
    loads[2][0].wait()
    forward(INNER)
    halo_start(fu.at[1], 1)
    shift_inner(fu.at[1])
    loads[3][0].wait()
    backward(INNER)
    for f in range(2):
        halo_zero(fu.at[f])
        halo_zero(hq.at[f])
    for g in range(2):
        part[g, :, :, :, 27] = jnp.zeros((2, 4, 2, 8, C), F32)
    halo_wait(fu.at[0], 0)
    shift_rim(fu.at[0])
    forward(RIM)
    halo_start(hq.at[0], 2)
    halo_wait(fu.at[1], 1)
    shift_rim(fu.at[1])
    turn(hq.at[0])
    wgrad(1, 0, fu.at[1], True)
    wgrad(1, 1, fu.at[1], True)
    wgrad(1, 2, fu.at[1], True)
    step0(1, 0)
    wgrad(1, 3, fu.at[1], True)
    step0(1, 1)
    backward(RIM)
    halo_start(hq.at[1], 3)
    step0(1, 2)
    step0(1, 3)
    turn(hq.at[1])
    wgrad(0, 0, fu.at[0], False)
    wgrad(0, 1, fu.at[0], False)
    wgrad(0, 2, fu.at[0], False)
    step0(0, 0)
    wgrad(0, 3, fu.at[0], False)
    step0(0, 1)
    shift_inner(hq.at[0])
    step0(0, 2)
    step0(0, 3)
    step(1, 0, 1)
    step(1, 1, 1)
    halo_wait(hq.at[0], 2)
    shift_rim(hq.at[0])
    finish(0, w2, False, FRONT)
    step(1, 2, 1)
    step(1, 3, 1)
    finish(0, w2, False, BACK)
    out_copy = pltpu.make_async_copy(outs.at[0], out_hbm, out_sem.at[0])
    out_copy.start()
    shift_inner(hq.at[1])
    step(0, 0, 1)
    step(0, 1, 1)
    halo_wait(hq.at[1], 3)
    shift_rim(hq.at[1])
    finish(1, w1, True, FRONT)
    step(0, 2, 1)
    step(0, 3, 1)
    step(1, 0, 2)
    step(1, 1, 2)
    step(1, 2, 2)
    step(1, 3, 2)
    finish(1, w1, True, BACK)
    gf_copy = pltpu.make_async_copy(outs.at[1], gf_hbm, out_sem.at[1])
    gf_copy.start()
    step(0, 0, 2)
    step(0, 1, 2)
    step(0, 2, 2)
    step(0, 3, 2)
    step(1, 0, 3)
    step(1, 1, 3)
    step(1, 2, 3)
    step(1, 3, 3)
    spread(1)
    settle(1)
    step(0, 0, 3)
    step(0, 1, 3)
    step(0, 2, 3)
    step(0, 3, 3)
    spread(0)
    g2_copy = collect(1, g2_hbm, 2)
    for slot, field in enumerate((fu.at[0], fu.at[1], hq.at[0], hq.at[1])):
        halo_sent(field, slot)
    settle(0)
    out_copy.wait()
    gf_copy.wait()
    g1_copy = collect(0, g1_hbm, 3)

    for g in range(2):
        seven(g).wait_send()
    for copy in (g2_copy, g1_copy):
        copy.wait()


def hand_on(*refs):
    sources, targets, sems = refs[:4], refs[4:8], refs[8]
    copies = [
        pltpu.make_async_copy(source, target, sems.at[i])
        for i, (source, target) in enumerate(zip(sources, targets))
    ]
    for copy in copies:
        copy.start()
    for copy in copies:
        copy.wait()


def body(features, w_first, w_second, occupancy, cotangent):
    scale = 1.0 / math.sqrt(GX * GY * X * Y * Z)
    anyspace = pl.BlockSpec(memory_space=pl.ANY)
    dma = pltpu.SemaphoreType.DMA
    vm = pltpu.VMEM
    split = (X, 8, 2, Z, C)
    field = (2, 3, X + 2, 10, 2, Z, C)
    tile = (8, C)
    scratch = {
        "feat": vm(split, BF16),
        "cot": vm(split, BF16),
        "w1": vm((27, C, C), BF16),
        "w2": vm((27, C, C), BF16),
        "fu": vm(field, BF16),
        "hq": vm(field, BF16),
        "slope": vm((X, 8, Z, 2 * C), F32),
        "at": vm((2, X, C, 8 * Z), BF16),
        "outs": vm((2, *split), BF16),
        "part": vm((2, 2, 4, 2, TAPS, *tile), F32),
        "r0": vm((2, 4, 2, TAPS, *tile), F32),
        "fin": vm((2, 4, *tile), F32),
        "rfin": vm((2, 7, 4, *tile), F32),
        "done": vm((2, TAPS, *tile), F32),
        "occ_here": pltpu.SMEM((1, 2, 2), jnp.int32),
        "occ_sem": dma((1,)),
        "in_sem": dma((4, 4)),
        "out_sem": dma((4,)),
        "hs": dma((4, 8)),
        "hr": dma((4, 8)),
        "s0s": dma((2, 4)),
        "s0r": dma((2, 4)),
        "rss": dma((2, 4, 3)),
        "rsr": dma((2, 4, 3)),
        "s4s": dma((2,)),
        "s4r": dma((2,)),
    }
    for p, part in enumerate(PARTS):
        scratch[f"h{p}"] = vm((2, *shape_of(part[1])), BF16)
        for stage in range(4):
            shape = shape_of(dims_after(part, stage))
            if stage < 3:
                scratch[f"t{p}_{stage}"] = vm((2, *shape), F32)
            if stage > 0:
                scratch[f"r{p}_{stage}"] = vm((2, 3, *shape), BF16 if stage == 1 else F32)
    names = ("occ", "f_in", "c_in", "w1_in", "w2_in", "out", "gf", "g1", "g2", *scratch)
    shapes = (
        jax.ShapeDtypeStruct(split, BF16),
        jax.ShapeDtypeStruct(split, BF16),
        jax.ShapeDtypeStruct((27, 8, C), F32),
        jax.ShapeDtypeStruct((27, 8, C), F32),
    )
    stay = [
        pltpu.with_memory_space_constraint(a, pltpu.HBM)
        for a in (occupancy, features.reshape(split), cotangent.reshape(split), w_first, w_second)
    ]
    results = pl.pallas_call(
        functools.partial(kernel, scale, names),
        name="section",
        out_shape=shapes,
        in_specs=[pl.BlockSpec(memory_space=pltpu.HBM)] * 5,
        out_specs=(anyspace,) * 4,
        scratch_shapes=list(scratch.values()),
        compiler_params=pltpu.CompilerParams(
            collective_id=0, has_side_effects=True, vmem_limit_bytes=48 * 2**20
        ),
    )(*stay)
    out, grad, first, second = pl.pallas_call(
        hand_on,
        name="hand_on",
        out_shape=shapes,
        in_specs=[anyspace] * 4,
        out_specs=(anyspace,) * 4,
        scratch_shapes=[dma((4,))],
        compiler_params=pltpu.CompilerParams(vmem_limit_bytes=8 * 2**20),
    )(*results)
    return out.reshape(features.shape), grad.reshape(features.shape), first, second


def solution(mesh):
    in_specs = (P("gx", "gy", None, None), P(), P(), P("gx", "gy", None), P("gx", "gy", None, None))
    out_specs = (
        P("gx", "gy", None, None),
        P("gx", "gy", None, None),
        P(None, "gy", None),
        P(None, "gy", None),
    )
    return jax.shard_map(body, mesh=mesh, in_specs=in_specs, out_specs=out_specs, check_vma=False)
```

```python
import functools
import math

import jax
import jax.numpy as jnp
from jax import lax
from jax.experimental import pallas as pl
from jax.experimental.pallas import tpu as pltpu
from jax.sharding import PartitionSpec as P

F32 = jnp.float32
BF16 = jnp.bfloat16
MESH = pl.DeviceIdType.MESH
DIRS = [(ax, ay) for ax in (-1, 0, 1) for ay in (-1, 0, 1) if (ax, ay) != (0, 0)]
GX, GY = 8, 16
X, Y, Z, C = 8, 16, 16, 128
TAPS = 28
HALVES = [(0, 4, 0, 8)], [(4, 4, 0, 8)]
FRONT = [(0, 2, 0, 8)], [(2, 2, 0, 8)]
BACK = [(4, 2, 0, 8)], [(6, 2, 0, 8)]
INNER = [(1, 3, 1, 6)], [(4, 3, 1, 6)]
RIM = [(0, 1, 0, 8), (1, 6, 0, 1)], [(7, 1, 0, 8), (1, 6, 7, 1)]

FULL = ("x", "yh", "z", "yl")
SIZE = {"x": 4, "yh": 2, "z": 4, "yl": 2}
PARTS = (
    (0, FULL, ("x", "z", "y")),
    (8, FULL, ("y", "x", "z")),
    (16, FULL, ("z", "y", "x")),
    (24, FULL[:3], ("x", "y", "z")),
)


PAIRS = sorted(
    ((i, j) for i in range(4) for j in range(4) if i or j), key=lambda d: -min(d[0], 4 - d[0]) - min(d[1], 4 - d[1])
)


def without(dims, axis):
    gone = ("yh", "yl") if axis == "y" else (axis,)
    return tuple(d for d in dims if d not in gone)


def dims_after(part, stages):
    dims = part[1]
    for axis in part[2][:stages]:
        dims = without(dims, axis)
    return dims


def shape_of(dims):
    return tuple(SIZE[d] for d in dims) + (8, C)


def kernel(scale, names, *refs):
    ref = dict(zip(names, refs))
    occ_hbm, feat_hbm, cot_hbm, w1_hbm, w2_hbm = (ref[n] for n in ("occ", "f_in", "c_in", "w1_in", "w2_in"))
    out_hbm, gf_hbm, g1_hbm, g2_hbm = (ref[n] for n in ("out", "gf", "g1", "g2"))
    feat, cot, w1, w2, fu, hq = (ref[n] for n in ("feat", "cot", "w1", "w2", "fu", "hq"))
    slope, at, outs, part, r0, fin, rfin, done = (
        ref[n] for n in ("slope", "at", "outs", "part", "r0", "fin", "rfin", "done")
    )
    occ_ref, occ_sem = ref["occ_here"], ref["occ_sem"]
    in_sem, out_sem, hs, hr, sent, s0r, rsr, s4s, s4r = (
        ref[n] for n in ("in_sem", "out_sem", "hs", "hr", "sent", "s0r", "rsr", "s4s", "s4r")
    )
    gx = lax.axis_index("gx")
    gy = lax.axis_index("gy")
    core = gy % 2
    px = (gy // 2) % 4
    yh = gy // 8
    pz = gx % 4
    yl = gx // 4
    py = yh * 2 + yl

    def at_x(k):
        return (px + k) % 4

    def at_y(k):
        return (py + k) % 4

    def at_z(k):
        return (pz + k) % 4

    def device(x=0, y=0, z=0):
        to = at_y(y)
        return ((to % 2) * 4 + at_z(z), (to // 2) * 8 + at_x(x) * 2 + core)

    partner = (gx, gy + 1 - 2 * core)

    def exists(ax, ay):
        ok = None
        for step, pos, size in ((ax, gx, GX), (ay, gy, GY)):
            if step == 0:
                continue
            here = pos + 1 < size if step > 0 else pos > 0
            ok = here if ok is None else jnp.logical_and(ok, here)
        return ok

    get_occ = pltpu.make_async_copy(occ_hbm, occ_ref, occ_sem.at[0])
    get_occ.start()
    loads = [
        [
            pltpu.make_async_copy(src.at[pl.ds(2 * i, 2)], dst.at[pl.ds(2 * i, 2)], in_sem.at[4 * f + i])
            for i in range(4)
        ]
        for f, (src, dst) in enumerate(((feat_hbm, feat), (cot_hbm, cot)))
    ]
    loads += [
        [pltpu.make_async_copy(src, dst, in_sem.at[f])] for f, src, dst in ((8, w1_hbm, w1), (9, w2_hbm, w2))
    ]
    for group in loads:
        for load in group:
            load.start()
    barrier = pltpu.get_barrier_semaphore()
    fixed = [partner]
    for axis in "xyz":
        fixed += [device(**{axis: k}) for k in (1, 2, 3)]
    for peer in fixed:
        pl.semaphore_signal(barrier, inc=1, device_id=peer, device_id_type=MESH)
    for ax, ay in DIRS:
        @pl.when(exists(ax, ay))
        def _():
            pl.semaphore_signal(barrier, inc=1, device_id=(gx + ax, gy + ay), device_id_type=MESH)

    get_occ.wait()
    low = lax.broadcasted_iota(jnp.int32, (Z, C), 0) < 8
    mask = [
        jnp.where(low, occ_ref[0, b, 0].astype(F32), occ_ref[0, b, 1].astype(F32)) for b in range(2)
    ]

    def mask_rows(boxes, wide):
        rows = []
        for x0, nx, k0, nk in boxes:
            for _ in range(nx):
                rows += [mask[k // 4] for k in range(k0, k0 + nk)]
        m = jnp.concatenate(rows, axis=0)
        return jnp.concatenate([m, m], axis=1) if wide else m

    def z_shift(field, at_index):
        v = field[(1, *at_index)].astype(F32)
        t = v.reshape(-1, Z, C)
        z = lax.broadcasted_iota(jnp.int32, (1, Z, C), 1)
        down = jnp.where(z == 0, 0.0, pltpu.roll(t, 1, 1))
        up = jnp.where(z == Z - 1, 0.0, pltpu.roll(t, Z - 1, 1))
        field[(0, *at_index)] = down.astype(BF16).reshape(v.shape)
        field[(2, *at_index)] = up.astype(BF16).reshape(v.shape)

    def edge_x(step, recv):
        if step == 0:
            return (pl.ds(1, X),)
        if recv:
            return (0 if step > 0 else X + 1,)
        return (X if step > 0 else 1,)

    def edge_y(step, recv):
        if step == 0:
            return (pl.ds(1, 8),)
        if recv:
            return (0, 1) if step > 0 else (9, 0)
        return (8, 1) if step > 0 else (1, 0)

    def halo_copy(ref, d, slot):
        ax, ay = DIRS[d]
        return pltpu.make_async_remote_copy(
            src_ref=ref.at[(1, *edge_x(ax, False), *edge_y(ay, False))],
            dst_ref=ref.at[(1, *edge_x(ax, True), *edge_y(ay, True))],
            send_sem=hs.at[slot % 2, d],
            recv_sem=hr.at[slot, d],
            device_id=(gx + ax, gy + ay),
            device_id_type=MESH,
        )

    def halo_start(ref, slot):
        for d, (ax, ay) in enumerate(DIRS):
            @pl.when(exists(ax, ay))
            def _():
                halo_copy(ref, d, slot).start()

    def halo_zero(ref):
        for ax, ay in DIRS:
            @pl.when(jnp.logical_not(exists(-ax, -ay)))
            def _():
                index = (1, *edge_x(ax, True), *edge_y(ay, True))
                ref[index] = jnp.zeros(ref.at[index].shape, BF16)

    def halo_wait(ref, slot):
        for d, (ax, ay) in enumerate(DIRS):
            @pl.when(exists(-ax, -ay))
            def _():
                halo_copy(ref, d, slot).wait_recv()

    def halo_sent(ref, slot):
        for d, (ax, ay) in enumerate(DIRS):
            @pl.when(exists(ax, ay))
            def _():
                halo_copy(ref, d, slot).wait_send()

    def shift_rim(field):
        for x in (0, X + 1):
            z_shift(field, (x,))
        for edge in ((0, 1), (9, 0)):
            z_shift(field, (pl.ds(1, X), *edge))

    def shift_inner(field):
        for x in range(1, X + 1):
            z_shift(field, (x, pl.ds(1, 8)))

    def rows_of(field, boxes, dz, dx, j):
        halves = []
        for h in range(2):
            pieces = [
                field[dz, pl.ds(x0 + dx, nx), pl.ds(k0 + j + h, nk), 1 - h].reshape(nx * nk * Z, C)
                for x0, nx, k0, nk in boxes
            ]
            halves.append(jnp.concatenate(pieces, axis=0) if len(pieces) > 1 else pieces[0])
        return jnp.concatenate(halves, axis=1)

    zero = jnp.zeros((C, C), BF16)

    def conv(field, w, boxes, flipped, planes=(0, 1, 2)):
        left, right = [], []
        for dx in planes:
            for dz in range(3):
                tap = [w[26 - (9 * dx + 3 * dy + dz)] if flipped else w[9 * dx + 3 * dy + dz] for dy in range(3)]
                for j in range(2):
                    left.append(rows_of(field, boxes, dz, dx, j))
                    if j == 0:
                        grid = ((tap[0], zero), (tap[1], tap[0]))
                    else:
                        grid = ((tap[2], tap[1]), (zero, tap[2]))
                    if flipped:
                        grid = tuple(zip(*grid))
                        right.append(jnp.concatenate([jnp.concatenate(r, axis=1) for r in grid], axis=0))
                    else:
                        right.append(jnp.concatenate([jnp.concatenate(r, axis=1) for r in grid], axis=0))
        lhs = jnp.concatenate(left, axis=1)
        if flipped:
            return lax.dot_general(
                lhs, jnp.concatenate(right, axis=1), (((1,), (1,)), ((), ())), preferred_element_type=F32
            )
        return jnp.dot(lhs, jnp.concatenate(right, axis=0), preferred_element_type=F32)

    def tiles(boxes):
        at_row = 0
        for x0, nx, k0, nk in boxes:
            n = nx * nk * Z
            yield (x0, nx, k0, nk), slice(at_row, at_row + n)
            at_row += n

    def put(field_at, boxes, value):
        for (x0, nx, k0, nk), rows in tiles(boxes):
            for h in range(2):
                field_at(x0, nx, k0, nk, h, value[rows, h * C : (h + 1) * C].reshape(nx, nk, Z, C))

    def put_padded(field):
        def store(x0, nx, k0, nk, h, v):
            field[1, pl.ds(x0 + 1, nx), pl.ds(k0 + 1, nk), h] = v.astype(BF16)
        return store

    def forward(pair):
        pres = [conv(fu.at[0], w1, boxes, False) for boxes in pair]
        for pre, boxes in zip(pres, pair):
            s = jax.nn.sigmoid(pre)
            m = mask_rows(boxes, True)
            put(put_padded(hq.at[0]), boxes, m * (pre * s))
            d = m * (s * (1.0 + pre * (1.0 - s)))
            for (x0, nx, k0, nk), rows in tiles(boxes):
                slope[pl.ds(x0, nx), pl.ds(k0, nk)] = d[rows].reshape(nx, nk, Z, 2 * C)

    def backward(pair):
        grads = [conv(fu.at[1], w2, boxes, True) for boxes in pair]
        for grad, boxes in zip(grads, pair):
            d = [slope[pl.ds(x0, nx), pl.ds(k0, nk)].reshape(nx * nk * Z, 2 * C) for x0, nx, k0, nk in boxes]
            d = jnp.concatenate(d, axis=0) if len(d) > 1 else d[0]
            put(put_padded(hq.at[1]), boxes, grad * d)

    def begin(slot, w, flipped, plane):
        sums = [conv(hq.at[slot], w, boxes, flipped, (plane,)) for boxes in HALVES]
        for total, (box,) in zip(sums, HALVES):
            x0, nx = box[:2]
            value = total.reshape(nx, 8, Z, 2 * C)
            slope[pl.ds(x0, nx)] = value if plane == 0 else slope[pl.ds(x0, nx)] + value

    def finish(slot, w, flipped, pair, planes=(0, 1, 2)):
        accs = [conv(hq.at[slot], w, boxes, flipped, planes) for boxes in pair]
        base = fu.at[slot]
        if len(planes) < 3:
            accs = [
                acc + slope[pl.ds(x0, nx)].reshape(nx * 8 * Z, 2 * C)
                for acc, ((x0, nx, _, _),) in zip(accs, pair)
            ]

        def store(x0, nx, k0, nk, h, v):
            b = base[1, pl.ds(x0 + 1, nx), pl.ds(k0 + 1, nk), h].astype(F32)
            outs[slot, pl.ds(x0, nx), pl.ds(k0, nk), h] = (b + v).astype(BF16)
        for acc, boxes in zip(accs, pair):
            put(store, boxes, acc * mask_rows(boxes, True))

    def turn(left):
        for h in range(2):
            for x in range(X):
                at[h, x] = left[1, x + 1, pl.ds(1, 8), h].reshape(8 * Z, C).T

    def wgrad(g, p, right, mirrored):
        lhs = jnp.concatenate([at[h, x] for h in range(2) for x in range(X)], axis=1)
        first = PARTS[p][0]
        middle = first + 4 if p < 3 else first + 2
        pair = range(first, middle), range(middle, min(first + 8, 27))
        sums = []
        for taps in pair:
            cols = []
            for tap in taps:
                dx, dy, dz = tap // 9, tap // 3 % 3, tap % 3
                ex, ey, ez = (2 - dx, 2 - dy, 2 - dz) if mirrored else (dx, dy, dz)
                halves = []
                for h in range(2):
                    row = h + ey + 1
                    halves.append(right[ez, pl.ds(ex, X), pl.ds(row // 2, 8), row % 2].reshape(X * 8 * Z, C))
                cols.append(jnp.concatenate(halves, axis=0))
            rhs = jnp.concatenate(cols, axis=1) if len(cols) > 1 else cols[0]
            sums.append(jnp.dot(lhs, rhs, preferred_element_type=F32))
        for acc, taps in zip(sums, pair):
            for i, tap in enumerate(taps):
                block = acc[:, i * C : (i + 1) * C]
                if not mirrored:
                    block = block.T
                for s in range(16):
                    part[g, s % 2, (s // 2) % 4, s // 8, tap] = block[8 * s : 8 * s + 8]
        start(stage0(g, p))

    def remote(src, dst, send, recv, to):
        return pltpu.make_async_remote_copy(
            src_ref=src, dst_ref=dst, send_sem=send, recv_sem=recv, device_id=to, device_id_type=MESH
        )

    def count(p):
        return 8 if p < 3 else 4

    def stage0(g, p):
        taps = pl.ds(PARTS[p][0], count(p))
        return [
            remote(
                part.at[g, 1 - core, :, :, taps], r0.at[g, :, :, taps], sent.at[g, p], s0r.at[g, p], partner
            )
        ]

    def pick(dims, where):
        index = []
        for d in dims:
            if d in where:
                index.append(where[d])
            elif d == "yh" and "y" in where:
                index.append(where["y"] // 2)
            elif d == "yl" and "y" in where:
                index.append(where["y"] % 2)
            else:
                index.append(slice(None))
        return tuple(index)

    position = {"x": at_x, "y": at_y, "z": at_z}

    def ring(g, p, stage):
        dims = dims_after(PARTS[p], stage - 1)
        axes = PARTS[p][2][:1] if stage == 1 else PARTS[p][2][1:]
        source = ref[f"h{p}"] if stage == 1 else ref[f"t{p}_1"]
        steps = [(k,) for k in (2, 1, 3)] if stage == 1 else PAIRS
        copies = []
        for n, away in enumerate(steps):
            where = {axis: position[axis](k) for axis, k in zip(axes, away)}
            copies.append(
                remote(
                    source.at[(g, *pick(dims, where))],
                    ref[f"r{p}_{stage}"].at[g, n],
                    sent.at[g, p],
                    rsr.at[g, p, stage - 1],
                    device(**dict(zip(axes, away))),
                )
            )
        return copies

    def three(g, p, stage):
        every = ref[f"r{p}_{stage}"].at[g]
        return remote(every, every, sent.at[g, p], rsr.at[g, p, stage - 1], partner)

    away = ((2, 1), (2, 0), (1, 1), (3, 1), (1, 0), (3, 0), (0, 1))

    def gather(g):
        return [
            remote(
                fin.at[g], rfin.at[g, i], s4s.at[g], s4r.at[g], ((yl + dy) % 2 * 4 + (pz + dz) % 4, gy)
            )
            for i, (dz, dy) in enumerate(away)
        ]

    def seven(g):
        return remote(rfin.at[g], rfin.at[g], s4s.at[g], s4r.at[g], partner)

    def start(copies):
        for copy in copies:
            copy.start()

    def arrive(copies):
        for copy in copies:
            copy.wait_recv()

    def step0(g, p):
        arrive(stage0(g, p))
        first = PARTS[p][0]
        for i in range(count(p)):
            total = part[g, core, :, :, first + i] + r0[g, :, :, first + i]
            index = (g, slice(None), slice(None)) + ((i // 2, i % 2) if p < 3 else (i,))
            ref[f"t{p}_0"][index] = total
            ref[f"h{p}"][index] = total.astype(BF16)
        stage0(g, p)[0].wait_send()
        start(ring(g, p, 1))

    def step(g, p, stage, arrived=False):
        if not arrived:
            three(g, p, stage).wait_recv()
        dims = dims_after(PARTS[p], stage - 1)
        axes = PARTS[p][2][:1] if stage == 1 else PARTS[p][2][1:]
        own = ref[f"t{p}_{stage - 1}"][(g, *pick(dims, {axis: position[axis](0) for axis in axes}))]
        r = ref[f"r{p}_{stage}"]
        if stage == 1:
            total = (own + r[g, 0].astype(F32)) + (r[g, 1].astype(F32) + r[g, 2].astype(F32))
            ref[f"t{p}_1"][g] = total
            three(g, p, 1).wait_send()
            start(ring(g, p, 2))
        else:
            terms = [own] + [r[g, n] for n in range(len(PAIRS))]
            while len(terms) > 1:
                terms = [a + b for a, b in zip(terms[::2], terms[1::2])]
            fin[g, p] = terms[0]

    def settle(g):
        for p in range(4):
            three(g, p, 2).wait_send()

    def spread(g):
        start(gather(g))

    def collect(g, target, sem):
        for p in range(3):
            done[g, 8 * p + 2 * pz + yl] = fin[g, p] * scale

        @pl.when(yl == 0)
        def _():
            done[g, 24 + pz] = fin[g, 3] * scale
        seven(g).wait_recv()
        for i, (dz, dy) in enumerate(away):
            z = (pz + 4 - dz) % 4
            low_y = (yl + dy) % 2
            for p in range(3):
                done[g, 8 * p + 2 * z + low_y] = rfin[g, i, p] * scale

            @pl.when(low_y == 0)
            def _():
                done[g, 24 + z] = rfin[g, i, 3] * scale
        copy = pltpu.make_async_copy(done.at[g, pl.ds(0, 27)], target, out_sem.at[sem])
        copy.start()
        return copy

    for f, raw in enumerate((feat, cot)):
        for x in range(X):
            if x % 2 == 0:
                loads[f][x // 2].wait()
            for b in range(2):
                rows = raw[x, pl.ds(4 * b, 4)].astype(F32) * mask[b][None, None]
                fu[f, 1, x + 1, pl.ds(4 * b + 1, 4)] = rows.astype(BF16)
    wide_x = 1 + (gx > 0).astype(jnp.int32) + (gx < GX - 1).astype(jnp.int32)
    wide_y = 1 + (gy > 0).astype(jnp.int32) + (gy < GY - 1).astype(jnp.int32)
    pl.semaphore_wait(barrier, len(fixed) + wide_x * wide_y - 1)

    halo_start(fu.at[0], 0)
    shift_inner(fu.at[0])
    loads[2][0].wait()
    forward(INNER)
    halo_start(fu.at[1], 1)
    shift_inner(fu.at[1])
    loads[3][0].wait()
    backward(INNER)
    for f in range(2):
        halo_zero(fu.at[f])
        halo_zero(hq.at[f])
    for g in range(2):
        part[g, :, :, :, 27] = jnp.zeros((2, 4, 2, 8, C), F32)
    halo_wait(fu.at[0], 0)
    shift_rim(fu.at[0])
    forward(RIM)
    halo_sent(fu.at[0], 0)
    halo_start(hq.at[0], 2)
    halo_wait(fu.at[1], 1)
    shift_rim(fu.at[1])
    turn(hq.at[0])
    wgrad(1, 0, fu.at[1], True)
    wgrad(1, 1, fu.at[1], True)
    wgrad(1, 2, fu.at[1], True)
    step0(1, 0)
    wgrad(1, 3, fu.at[1], True)
    step0(1, 1)
    backward(RIM)
    step0(1, 2)
    step0(1, 3)
    halo_sent(fu.at[1], 1)
    halo_start(hq.at[1], 3)
    turn(hq.at[1])
    wgrad(0, 0, fu.at[0], False)
    wgrad(0, 1, fu.at[0], False)
    wgrad(0, 2, fu.at[0], False)
    step0(0, 0)
    wgrad(0, 3, fu.at[0], False)
    step0(0, 1)
    shift_inner(hq.at[0])
    step0(0, 2)
    step0(0, 3)
    halo_wait(hq.at[0], 2)
    shift_rim(hq.at[0])
    finish(0, w2, False, FRONT)
    for p in range(4):
        three(1, p, 1).wait_recv()
    for p in range(4):
        step(1, p, 1, True)
    finish(0, w2, False, BACK)
    out_copy = pltpu.make_async_copy(outs.at[0], out_hbm, out_sem.at[0])
    out_copy.start()
    shift_inner(hq.at[1])
    step(0, 0, 1)
    step(0, 1, 1)
    halo_wait(hq.at[1], 3)
    shift_rim(hq.at[1])
    begin(1, w1, True, 0)
    step(0, 2, 1)
    step(0, 3, 1)
    begin(1, w1, True, 1)
    step(1, 0, 2)
    step(1, 1, 2)
    step(1, 2, 2)
    step(1, 3, 2)
    spread(1)
    finish(1, w1, True, HALVES, (2,))
    gf_copy = pltpu.make_async_copy(outs.at[1], gf_hbm, out_sem.at[1])
    gf_copy.start()
    settle(1)
    step(0, 0, 2)
    step(0, 1, 2)
    step(0, 2, 2)
    step(0, 3, 2)
    spread(0)
    g2_copy = collect(1, g2_hbm, 2)
    halo_sent(hq.at[0], 2)
    halo_sent(hq.at[1], 3)
    settle(0)
    out_copy.wait()
    gf_copy.wait()
    g1_copy = collect(0, g1_hbm, 3)

    for g in range(2):
        seven(g).wait_send()
    for copy in (g2_copy, g1_copy):
        copy.wait()


def hand_on(*refs):
    sources, targets, sems = refs[:4], refs[4:8], refs[8]
    copies = [
        pltpu.make_async_copy(source, target, sems.at[i])
        for i, (source, target) in enumerate(zip(sources, targets))
    ]
    for copy in copies:
        copy.start()
    for copy in copies:
        copy.wait()


def body(features, w_first, w_second, occupancy, cotangent):
    scale = 1.0 / math.sqrt(GX * GY * X * Y * Z)
    anyspace = pl.BlockSpec(memory_space=pl.ANY)
    dma = pltpu.SemaphoreType.DMA
    vm = pltpu.VMEM
    split = (X, 8, 2, Z, C)
    field = (2, 3, X + 2, 10, 2, Z, C)
    tile = (8, C)
    scratch = {
        "feat": vm(split, BF16),
        "cot": vm(split, BF16),
        "w1": vm((27, C, C), BF16),
        "w2": vm((27, C, C), BF16),
        "fu": vm(field, BF16),
        "hq": vm(field, BF16),
        "slope": vm((X, 8, Z, 2 * C), F32),
        "at": vm((2, X, C, 8 * Z), BF16),
        "outs": vm((2, *split), BF16),
        "part": vm((2, 2, 4, 2, TAPS, *tile), F32),
        "r0": vm((2, 4, 2, TAPS, *tile), F32),
        "fin": vm((2, 4, *tile), F32),
        "rfin": vm((2, 7, 4, *tile), F32),
        "done": vm((2, TAPS, *tile), F32),
        "occ_here": pltpu.SMEM((1, 2, 2), jnp.int32),
        "occ_sem": dma((1,)),
        "in_sem": dma((10,)),
        "out_sem": dma((4,)),
        "hs": dma((2, 8)),
        "hr": dma((4, 8)),
        "sent": dma((2, 4)),
        "s0r": dma((2, 4)),
        "rsr": dma((2, 4, 2)),
        "s4s": dma((2,)),
        "s4r": dma((2,)),
    }
    for p, part in enumerate(PARTS):
        scratch[f"h{p}"] = vm((2, *shape_of(part[1])), BF16)
        for stage in range(2):
            shape = shape_of(dims_after(part, stage))
            scratch[f"t{p}_{stage}"] = vm((2, *shape), F32)
        scratch[f"r{p}_1"] = vm((2, 3, *shape_of(dims_after(part, 1))), BF16)
        scratch[f"r{p}_2"] = vm((2, len(PAIRS), *tile), F32)
    names = ("occ", "f_in", "c_in", "w1_in", "w2_in", "out", "gf", "g1", "g2", *scratch)
    shapes = (
        jax.ShapeDtypeStruct(split, BF16),
        jax.ShapeDtypeStruct(split, BF16),
        jax.ShapeDtypeStruct((27, 8, C), F32),
        jax.ShapeDtypeStruct((27, 8, C), F32),
    )
    stay = [
        pltpu.with_memory_space_constraint(a, pltpu.HBM)
        for a in (occupancy, features.reshape(split), cotangent.reshape(split), w_first, w_second)
    ]
    results = pl.pallas_call(
        functools.partial(kernel, scale, names),
        name="section",
        out_shape=shapes,
        in_specs=[pl.BlockSpec(memory_space=pltpu.HBM)] * 5,
        out_specs=(anyspace,) * 4,
        scratch_shapes=list(scratch.values()),
        compiler_params=pltpu.CompilerParams(
            collective_id=0, has_side_effects=True, vmem_limit_bytes=48 * 2**20
        ),
    )(*stay)
    out, grad, first, second = pl.pallas_call(
        hand_on,
        name="hand_on",
        out_shape=shapes,
        in_specs=[anyspace] * 4,
        out_specs=(anyspace,) * 4,
        scratch_shapes=[dma((4,))],
        compiler_params=pltpu.CompilerParams(vmem_limit_bytes=8 * 2**20),
    )(*results)
    return out.reshape(features.shape), grad.reshape(features.shape), first, second


def solution(mesh):
    in_specs = (P("gx", "gy", None, None), P(), P(), P("gx", "gy", None), P("gx", "gy", None, None))
    out_specs = (
        P("gx", "gy", None, None),
        P("gx", "gy", None, None),
        P(None, "gy", None),
        P(None, "gy", None),
    )
    return jax.shard_map(body, mesh=mesh, in_specs=in_specs, out_specs=out_specs, check_vma=False)
```

```python
import functools
import math

import jax
import jax.numpy as jnp
from jax import lax
from jax.experimental import pallas as pl
from jax.experimental.pallas import tpu as pltpu
from jax.sharding import PartitionSpec as P

F32 = jnp.float32
BF16 = jnp.bfloat16
MESH = pl.DeviceIdType.MESH
DIRS = [(ax, ay) for ax in (-1, 0, 1) for ay in (-1, 0, 1) if (ax, ay) != (0, 0)]
GX, GY = 8, 16
X, Y, Z, C = 8, 16, 16, 128
TAPS = 28
HALVES = [(0, 4, 0, 8)], [(4, 4, 0, 8)]
FRONT = [(0, 2, 0, 8)], [(2, 2, 0, 8)]
BACK = [(4, 2, 0, 8)], [(6, 2, 0, 8)]
INNER = [(1, 3, 1, 6)], [(4, 3, 1, 6)]
RIM = [(0, 1, 0, 8), (1, 6, 0, 1)], [(7, 1, 0, 8), (1, 6, 7, 1)]

FULL = ("x", "yh", "z", "yl")
SIZE = {"x": 4, "yh": 2, "z": 4, "yl": 2}
PARTS = (
    (0, FULL, ("x", "z", "y")),
    (8, FULL, ("y", "x", "z")),
    (16, FULL, ("z", "y", "x")),
    (24, FULL[:3], ("x", "y", "z")),
)


PAIRS = sorted(
    ((i, j) for i in range(4) for j in range(4) if i or j), key=lambda d: -min(d[0], 4 - d[0]) - min(d[1], 4 - d[1])
)


def without(dims, axis):
    gone = ("yh", "yl") if axis == "y" else (axis,)
    return tuple(d for d in dims if d not in gone)


def dims_after(part, stages):
    dims = part[1]
    for axis in part[2][:stages]:
        dims = without(dims, axis)
    return dims


def shape_of(dims):
    return tuple(SIZE[d] for d in dims) + (8, C)


def kernel(scale, names, *refs):
    ref = dict(zip(names, refs))
    occ_hbm, feat_hbm, cot_hbm, w1_hbm, w2_hbm = (ref[n] for n in ("occ", "f_in", "c_in", "w1_in", "w2_in"))
    out_hbm, gf_hbm, g1_hbm, g2_hbm = (ref[n] for n in ("out", "gf", "g1", "g2"))
    feat, cot, w1, w2, fu, hq = (ref[n] for n in ("feat", "cot", "w1", "w2", "fu", "hq"))
    slope, at, outs, part, r0, fin, rfin, done = (
        ref[n] for n in ("slope", "at", "outs", "part", "r0", "fin", "rfin", "done")
    )
    occ_ref, occ_sem = ref["occ_here"], ref["occ_sem"]
    in_sem, out_sem, hs, hr, sent, s0r, rsr, s4s, s4r = (
        ref[n] for n in ("in_sem", "out_sem", "hs", "hr", "sent", "s0r", "rsr", "s4s", "s4r")
    )
    gx = lax.axis_index("gx")
    gy = lax.axis_index("gy")
    core = gy % 2
    px = (gy // 2) % 4
    yh = gy // 8
    pz = gx % 4
    yl = gx // 4
    py = yh * 2 + yl

    def at_x(k):
        return (px + k) % 4

    def at_y(k):
        return (py + k) % 4

    def at_z(k):
        return (pz + k) % 4

    def device(x=0, y=0, z=0):
        to = at_y(y)
        return ((to % 2) * 4 + at_z(z), (to // 2) * 8 + at_x(x) * 2 + core)

    partner = (gx, gy + 1 - 2 * core)

    def exists(ax, ay):
        ok = None
        for step, pos, size in ((ax, gx, GX), (ay, gy, GY)):
            if step == 0:
                continue
            here = pos + 1 < size if step > 0 else pos > 0
            ok = here if ok is None else jnp.logical_and(ok, here)
        return ok

    get_occ = pltpu.make_async_copy(occ_hbm, occ_ref, occ_sem.at[0])
    get_occ.start()
    loads = [
        [
            pltpu.make_async_copy(src.at[pl.ds(2 * i, 2)], dst.at[pl.ds(2 * i, 2)], in_sem.at[4 * f + i])
            for i in range(4)
        ]
        for f, (src, dst) in enumerate(((feat_hbm, feat), (cot_hbm, cot)))
    ]
    loads += [
        [pltpu.make_async_copy(src, dst, in_sem.at[f])] for f, src, dst in ((8, w1_hbm, w1), (9, w2_hbm, w2))
    ]
    for group in loads:
        for load in group:
            load.start()
    barrier = pltpu.get_barrier_semaphore()
    fixed = [partner]
    for axis in "xyz":
        fixed += [device(**{axis: k}) for k in (1, 2, 3)]
    for peer in fixed:
        pl.semaphore_signal(barrier, inc=1, device_id=peer, device_id_type=MESH)
    for ax, ay in DIRS:
        @pl.when(exists(ax, ay))
        def _():
            pl.semaphore_signal(barrier, inc=1, device_id=(gx + ax, gy + ay), device_id_type=MESH)

    get_occ.wait()
    low = lax.broadcasted_iota(jnp.int32, (Z, C), 0) < 8
    mask = [
        jnp.where(low, occ_ref[0, b, 0].astype(F32), occ_ref[0, b, 1].astype(F32)) for b in range(2)
    ]

    def mask_rows(boxes, wide):
        rows = []
        for x0, nx, k0, nk in boxes:
            for _ in range(nx):
                rows += [mask[k // 4] for k in range(k0, k0 + nk)]
        m = jnp.concatenate(rows, axis=0)
        return jnp.concatenate([m, m], axis=1) if wide else m

    def z_shift(field, at_index):
        v = field[(1, *at_index)].astype(F32)
        t = v.reshape(-1, Z, C)
        z = lax.broadcasted_iota(jnp.int32, (1, Z, C), 1)
        down = jnp.where(z == 0, 0.0, pltpu.roll(t, 1, 1))
        up = jnp.where(z == Z - 1, 0.0, pltpu.roll(t, Z - 1, 1))
        field[(0, *at_index)] = down.astype(BF16).reshape(v.shape)
        field[(2, *at_index)] = up.astype(BF16).reshape(v.shape)

    def edge_x(step, recv):
        if step == 0:
            return (pl.ds(1, X),)
        if recv:
            return (0 if step > 0 else X + 1,)
        return (X if step > 0 else 1,)

    def edge_y(step, recv):
        if step == 0:
            return (pl.ds(1, 8),)
        if recv:
            return (0, 1) if step > 0 else (9, 0)
        return (8, 1) if step > 0 else (1, 0)

    def halo_copy(ref, d, slot):
        ax, ay = DIRS[d]
        return pltpu.make_async_remote_copy(
            src_ref=ref.at[(1, *edge_x(ax, False), *edge_y(ay, False))],
            dst_ref=ref.at[(1, *edge_x(ax, True), *edge_y(ay, True))],
            send_sem=hs.at[slot % 2, d],
            recv_sem=hr.at[slot, d],
            device_id=(gx + ax, gy + ay),
            device_id_type=MESH,
        )

    def halo_start(ref, slot):
        for d, (ax, ay) in enumerate(DIRS):
            @pl.when(exists(ax, ay))
            def _():
                halo_copy(ref, d, slot).start()

    def halo_zero(ref):
        for ax, ay in DIRS:
            @pl.when(jnp.logical_not(exists(-ax, -ay)))
            def _():
                index = (1, *edge_x(ax, True), *edge_y(ay, True))
                ref[index] = jnp.zeros(ref.at[index].shape, BF16)

    def halo_wait(ref, slot):
        for d, (ax, ay) in enumerate(DIRS):
            @pl.when(exists(-ax, -ay))
            def _():
                halo_copy(ref, d, slot).wait_recv()

    def halo_sent(ref, slot):
        for d, (ax, ay) in enumerate(DIRS):
            @pl.when(exists(ax, ay))
            def _():
                halo_copy(ref, d, slot).wait_send()

    def shift_rim(field):
        for x in (0, X + 1):
            z_shift(field, (x,))
        for edge in ((0, 1), (9, 0)):
            z_shift(field, (pl.ds(1, X), *edge))

    def shift_inner(field):
        for x in range(1, X + 1):
            z_shift(field, (x, pl.ds(1, 8)))

    def rows_of(field, boxes, dz, dx, j):
        halves = []
        for h in range(2):
            pieces = [
                field[dz, pl.ds(x0 + dx, nx), pl.ds(k0 + j + h, nk), 1 - h].reshape(nx * nk * Z, C)
                for x0, nx, k0, nk in boxes
            ]
            halves.append(jnp.concatenate(pieces, axis=0) if len(pieces) > 1 else pieces[0])
        return jnp.concatenate(halves, axis=1)

    zero = jnp.zeros((C, C), BF16)

    def conv(field, w, boxes, flipped, planes=(0, 1, 2)):
        left, right = [], []
        for dx in planes:
            for dz in range(3):
                tap = [w[26 - (9 * dx + 3 * dy + dz)] if flipped else w[9 * dx + 3 * dy + dz] for dy in range(3)]
                for j in range(2):
                    left.append(rows_of(field, boxes, dz, dx, j))
                    if j == 0:
                        grid = ((tap[0], zero), (tap[1], tap[0]))
                    else:
                        grid = ((tap[2], tap[1]), (zero, tap[2]))
                    if flipped:
                        grid = tuple(zip(*grid))
                        right.append(jnp.concatenate([jnp.concatenate(r, axis=1) for r in grid], axis=0))
                    else:
                        right.append(jnp.concatenate([jnp.concatenate(r, axis=1) for r in grid], axis=0))
        lhs = jnp.concatenate(left, axis=1)
        if flipped:
            return lax.dot_general(
                lhs, jnp.concatenate(right, axis=1), (((1,), (1,)), ((), ())), preferred_element_type=F32
            )
        return jnp.dot(lhs, jnp.concatenate(right, axis=0), preferred_element_type=F32)

    def tiles(boxes):
        at_row = 0
        for x0, nx, k0, nk in boxes:
            n = nx * nk * Z
            yield (x0, nx, k0, nk), slice(at_row, at_row + n)
            at_row += n

    def put(field_at, boxes, value):
        for (x0, nx, k0, nk), rows in tiles(boxes):
            for h in range(2):
                field_at(x0, nx, k0, nk, h, value[rows, h * C : (h + 1) * C].reshape(nx, nk, Z, C))

    def put_padded(field):
        def store(x0, nx, k0, nk, h, v):
            field[1, pl.ds(x0 + 1, nx), pl.ds(k0 + 1, nk), h] = v.astype(BF16)
        return store

    def forward(pair):
        pres = [conv(fu.at[0], w1, boxes, False) for boxes in pair]
        for pre, boxes in zip(pres, pair):
            s = jax.nn.sigmoid(pre)
            m = mask_rows(boxes, True)
            put(put_padded(hq.at[0]), boxes, m * (pre * s))
            d = m * (s * (1.0 + pre * (1.0 - s)))
            for (x0, nx, k0, nk), rows in tiles(boxes):
                slope[pl.ds(x0, nx), pl.ds(k0, nk)] = d[rows].reshape(nx, nk, Z, 2 * C)

    def backward(pair):
        grads = [conv(fu.at[1], w2, boxes, True) for boxes in pair]
        for grad, boxes in zip(grads, pair):
            d = [slope[pl.ds(x0, nx), pl.ds(k0, nk)].reshape(nx * nk * Z, 2 * C) for x0, nx, k0, nk in boxes]
            d = jnp.concatenate(d, axis=0) if len(d) > 1 else d[0]
            put(put_padded(hq.at[1]), boxes, grad * d)

    def begin(slot, w, flipped, plane):
        sums = [conv(hq.at[slot], w, boxes, flipped, (plane,)) for boxes in HALVES]
        for total, (box,) in zip(sums, HALVES):
            x0, nx = box[:2]
            value = total.reshape(nx, 8, Z, 2 * C)
            slope[pl.ds(x0, nx)] = value if plane == 0 else slope[pl.ds(x0, nx)] + value

    def finish(slot, w, flipped, pair, planes=(0, 1, 2)):
        accs = [conv(hq.at[slot], w, boxes, flipped, planes) for boxes in pair]
        base = fu.at[slot]
        if len(planes) < 3:
            accs = [
                acc + slope[pl.ds(x0, nx)].reshape(nx * 8 * Z, 2 * C)
                for acc, ((x0, nx, _, _),) in zip(accs, pair)
            ]

        def store(x0, nx, k0, nk, h, v):
            b = base[1, pl.ds(x0 + 1, nx), pl.ds(k0 + 1, nk), h].astype(F32)
            outs[slot, pl.ds(x0, nx), pl.ds(k0, nk), h] = (b + v).astype(BF16)
        for acc, boxes in zip(accs, pair):
            put(store, boxes, acc * mask_rows(boxes, True))

    def turn(left):
        for h in range(2):
            for x in range(X):
                at[h, x] = left[1, x + 1, pl.ds(1, 8), h].reshape(8 * Z, C).T

    def wgrad(g, p, right, mirrored):
        lhs = jnp.concatenate([at[h, x] for h in range(2) for x in range(X)], axis=1)
        first = PARTS[p][0]
        middle = first + 4 if p < 3 else first + 2
        pair = range(first, middle), range(middle, min(first + 8, 27))
        sums = []
        for taps in pair:
            cols = []
            for tap in taps:
                dx, dy, dz = tap // 9, tap // 3 % 3, tap % 3
                ex, ey, ez = (2 - dx, 2 - dy, 2 - dz) if mirrored else (dx, dy, dz)
                halves = []
                for h in range(2):
                    row = h + ey + 1
                    halves.append(right[ez, pl.ds(ex, X), pl.ds(row // 2, 8), row % 2].reshape(X * 8 * Z, C))
                cols.append(jnp.concatenate(halves, axis=0))
            rhs = jnp.concatenate(cols, axis=1) if len(cols) > 1 else cols[0]
            sums.append(jnp.dot(lhs, rhs, preferred_element_type=F32))
        for acc, taps in zip(sums, pair):
            for i, tap in enumerate(taps):
                block = acc[:, i * C : (i + 1) * C]
                if not mirrored:
                    block = block.T
                for s in range(16):
                    part[g, s % 2, (s // 2) % 4, s // 8, tap] = block[8 * s : 8 * s + 8]
        start(stage0(g, p))

    def remote(src, dst, send, recv, to):
        return pltpu.make_async_remote_copy(
            src_ref=src, dst_ref=dst, send_sem=send, recv_sem=recv, device_id=to, device_id_type=MESH
        )

    def count(p):
        return 8 if p < 3 else 4

    def stage0(g, p):
        taps = pl.ds(PARTS[p][0], count(p))
        return [
            remote(
                part.at[g, 1 - core, :, :, taps], r0.at[g, :, :, taps], sent.at[g, p], s0r.at[g, p], partner
            )
        ]

    def pick(dims, where):
        index = []
        for d in dims:
            if d in where:
                index.append(where[d])
            elif d == "yh" and "y" in where:
                index.append(where["y"] // 2)
            elif d == "yl" and "y" in where:
                index.append(where["y"] % 2)
            else:
                index.append(slice(None))
        return tuple(index)

    position = {"x": at_x, "y": at_y, "z": at_z}

    def ring(g, p, stage):
        dims = dims_after(PARTS[p], stage - 1)
        axes = PARTS[p][2][:1] if stage == 1 else PARTS[p][2][1:]
        source = ref[f"h{p}"] if stage == 1 else ref[f"t{p}_1"]
        steps = [(k,) for k in (2, 1, 3)] if stage == 1 else PAIRS
        copies = []
        for n, away in enumerate(steps):
            where = {axis: position[axis](k) for axis, k in zip(axes, away)}
            copies.append(
                remote(
                    source.at[(g, *pick(dims, where))],
                    ref[f"r{p}_{stage}"].at[g, n],
                    sent.at[g, p],
                    rsr.at[g, p, stage - 1],
                    device(**dict(zip(axes, away))),
                )
            )
        return copies

    def three(g, p, stage):
        every = ref[f"r{p}_{stage}"].at[g]
        return remote(every, every, sent.at[g, p], rsr.at[g, p, stage - 1], partner)

    away = ((2, 1), (2, 0), (1, 1), (3, 1), (1, 0), (3, 0), (0, 1))

    def shares(late):
        return pl.ds(3, 1) if late else pl.ds(0, 3)

    def gather(g, late):
        return [
            remote(
                fin.at[g, shares(late)],
                rfin.at[g, i, shares(late)],
                s4s.at[g, late],
                s4r.at[g, late],
                ((yl + dy) % 2 * 4 + (pz + dz) % 4, gy),
            )
            for i, (dz, dy) in enumerate(away)
        ]

    def seven(g, late):
        every = rfin.at[g, :, shares(late)]
        return remote(every, every, s4s.at[g, late], s4r.at[g, late], partner)

    def start(copies):
        for copy in copies:
            copy.start()

    def arrive(copies):
        for copy in copies:
            copy.wait_recv()

    def step0(g, p):
        arrive(stage0(g, p))
        first = PARTS[p][0]
        for i in range(count(p)):
            total = part[g, core, :, :, first + i] + r0[g, :, :, first + i]
            index = (g, slice(None), slice(None)) + ((i // 2, i % 2) if p < 3 else (i,))
            ref[f"t{p}_0"][index] = total
            ref[f"h{p}"][index] = total.astype(BF16)
        stage0(g, p)[0].wait_send()
        start(ring(g, p, 1))

    def step(g, p, stage, arrived=False):
        if not arrived:
            three(g, p, stage).wait_recv()
        dims = dims_after(PARTS[p], stage - 1)
        axes = PARTS[p][2][:1] if stage == 1 else PARTS[p][2][1:]
        own = ref[f"t{p}_{stage - 1}"][(g, *pick(dims, {axis: position[axis](0) for axis in axes}))]
        r = ref[f"r{p}_{stage}"]
        if stage == 1:
            total = (own + r[g, 0].astype(F32)) + (r[g, 1].astype(F32) + r[g, 2].astype(F32))
            ref[f"t{p}_1"][g] = total
            three(g, p, 1).wait_send()
            start(ring(g, p, 2))
        else:
            terms = [own] + [r[g, n] for n in range(len(PAIRS))]
            while len(terms) > 1:
                terms = [a + b for a, b in zip(terms[::2], terms[1::2])]
            fin[g, p] = terms[0]

    def settle(g):
        for p in range(4):
            three(g, p, 2).wait_send()

    def spread(g, late):
        start(gather(g, late))

    def collect(g, target, sem):
        for p in range(3):
            done[g, 8 * p + 2 * pz + yl] = fin[g, p] * scale

        @pl.when(yl == 0)
        def _():
            done[g, 24 + pz] = fin[g, 3] * scale
        seven(g, 0).wait_recv()
        seven(g, 1).wait_recv()
        for i, (dz, dy) in enumerate(away):
            z = (pz + 4 - dz) % 4
            low_y = (yl + dy) % 2
            for p in range(3):
                done[g, 8 * p + 2 * z + low_y] = rfin[g, i, p] * scale

            @pl.when(low_y == 0)
            def _():
                done[g, 24 + z] = rfin[g, i, 3] * scale
        copy = pltpu.make_async_copy(done.at[g, pl.ds(0, 27)], target, out_sem.at[sem])
        copy.start()
        return copy

    for f, raw in enumerate((feat, cot)):
        for x in range(X):
            if x % 2 == 0:
                loads[f][x // 2].wait()
            for b in range(2):
                rows = raw[x, pl.ds(4 * b, 4)].astype(F32) * mask[b][None, None]
                fu[f, 1, x + 1, pl.ds(4 * b + 1, 4)] = rows.astype(BF16)
    wide_x = 1 + (gx > 0).astype(jnp.int32) + (gx < GX - 1).astype(jnp.int32)
    wide_y = 1 + (gy > 0).astype(jnp.int32) + (gy < GY - 1).astype(jnp.int32)
    pl.semaphore_wait(barrier, len(fixed) + wide_x * wide_y - 1)

    halo_start(fu.at[0], 0)
    shift_inner(fu.at[0])
    loads[2][0].wait()
    forward(INNER)
    halo_start(fu.at[1], 1)
    shift_inner(fu.at[1])
    loads[3][0].wait()
    backward(INNER)
    for f in range(2):
        halo_zero(fu.at[f])
        halo_zero(hq.at[f])
    for g in range(2):
        part[g, :, :, :, 27] = jnp.zeros((2, 4, 2, 8, C), F32)
    halo_wait(fu.at[0], 0)
    shift_rim(fu.at[0])
    forward(RIM)
    halo_sent(fu.at[0], 0)
    halo_start(hq.at[0], 2)
    halo_wait(fu.at[1], 1)
    shift_rim(fu.at[1])
    turn(hq.at[0])
    wgrad(1, 0, fu.at[1], True)
    wgrad(1, 1, fu.at[1], True)
    wgrad(1, 2, fu.at[1], True)
    step0(1, 0)
    wgrad(1, 3, fu.at[1], True)
    step0(1, 1)
    backward(RIM)
    step0(1, 2)
    step0(1, 3)
    halo_sent(fu.at[1], 1)
    halo_start(hq.at[1], 3)
    turn(hq.at[1])
    wgrad(0, 0, fu.at[0], False)
    wgrad(0, 1, fu.at[0], False)
    wgrad(0, 2, fu.at[0], False)
    step0(0, 0)
    wgrad(0, 3, fu.at[0], False)
    step0(0, 1)
    shift_inner(hq.at[0])
    step0(0, 2)
    step0(0, 3)
    halo_wait(hq.at[0], 2)
    shift_rim(hq.at[0])
    finish(0, w2, False, FRONT)
    for p in range(4):
        three(1, p, 1).wait_recv()
    for p in range(4):
        step(1, p, 1, True)
    finish(0, w2, False, BACK)
    out_copy = pltpu.make_async_copy(outs.at[0], out_hbm, out_sem.at[0])
    out_copy.start()
    shift_inner(hq.at[1])
    step(0, 0, 1)
    step(0, 1, 1)
    halo_wait(hq.at[1], 3)
    shift_rim(hq.at[1])
    begin(1, w1, True, 0)
    step(0, 2, 1)
    step(0, 3, 1)
    begin(1, w1, True, 1)
    finish(1, w1, True, HALVES, (2,))
    gf_copy = pltpu.make_async_copy(outs.at[1], gf_hbm, out_sem.at[1])
    gf_copy.start()
    step(1, 0, 2)
    step(1, 1, 2)
    step(1, 2, 2)
    spread(1, 0)
    step(1, 3, 2)
    spread(1, 1)
    settle(1)
    step(0, 0, 2)
    step(0, 1, 2)
    step(0, 2, 2)
    spread(0, 0)
    step(0, 3, 2)
    spread(0, 1)
    g2_copy = collect(1, g2_hbm, 2)
    halo_sent(hq.at[0], 2)
    halo_sent(hq.at[1], 3)
    settle(0)
    out_copy.wait()
    gf_copy.wait()
    g1_copy = collect(0, g1_hbm, 3)

    for g in range(2):
        seven(g, 0).wait_send()
        seven(g, 1).wait_send()
    for copy in (g2_copy, g1_copy):
        copy.wait()


def hand_on(*refs):
    sources, targets, sems = refs[:4], refs[4:8], refs[8]
    copies = [
        pltpu.make_async_copy(source, target, sems.at[i])
        for i, (source, target) in enumerate(zip(sources, targets))
    ]
    for copy in copies:
        copy.start()
    for copy in copies:
        copy.wait()


def body(features, w_first, w_second, occupancy, cotangent):
    scale = 1.0 / math.sqrt(GX * GY * X * Y * Z)
    anyspace = pl.BlockSpec(memory_space=pl.ANY)
    dma = pltpu.SemaphoreType.DMA
    vm = pltpu.VMEM
    split = (X, 8, 2, Z, C)
    field = (2, 3, X + 2, 10, 2, Z, C)
    tile = (8, C)
    scratch = {
        "feat": vm(split, BF16),
        "cot": vm(split, BF16),
        "w1": vm((27, C, C), BF16),
        "w2": vm((27, C, C), BF16),
        "fu": vm(field, BF16),
        "hq": vm(field, BF16),
        "slope": vm((X, 8, Z, 2 * C), F32),
        "at": vm((2, X, C, 8 * Z), BF16),
        "outs": vm((2, *split), BF16),
        "part": vm((2, 2, 4, 2, TAPS, *tile), F32),
        "r0": vm((2, 4, 2, TAPS, *tile), F32),
        "fin": vm((2, 4, *tile), F32),
        "rfin": vm((2, 7, 4, *tile), F32),
        "done": vm((2, TAPS, *tile), F32),
        "occ_here": pltpu.SMEM((1, 2, 2), jnp.int32),
        "occ_sem": dma((1,)),
        "in_sem": dma((10,)),
        "out_sem": dma((4,)),
        "hs": dma((2, 8)),
        "hr": dma((4, 8)),
        "sent": dma((2, 4)),
        "s0r": dma((2, 4)),
        "rsr": dma((2, 4, 2)),
        "s4s": dma((2, 2)),
        "s4r": dma((2, 2)),
    }
    for p, part in enumerate(PARTS):
        scratch[f"h{p}"] = vm((2, *shape_of(part[1])), BF16)
        for stage in range(2):
            shape = shape_of(dims_after(part, stage))
            scratch[f"t{p}_{stage}"] = vm((2, *shape), F32)
        scratch[f"r{p}_1"] = vm((2, 3, *shape_of(dims_after(part, 1))), BF16)
        scratch[f"r{p}_2"] = vm((2, len(PAIRS), *tile), F32)
    names = ("occ", "f_in", "c_in", "w1_in", "w2_in", "out", "gf", "g1", "g2", *scratch)
    shapes = (
        jax.ShapeDtypeStruct(split, BF16),
        jax.ShapeDtypeStruct(split, BF16),
        jax.ShapeDtypeStruct((27, 8, C), F32),
        jax.ShapeDtypeStruct((27, 8, C), F32),
    )
    stay = [
        pltpu.with_memory_space_constraint(a, pltpu.HBM)
        for a in (occupancy, features.reshape(split), cotangent.reshape(split), w_first, w_second)
    ]
    results = pl.pallas_call(
        functools.partial(kernel, scale, names),
        name="section",
        out_shape=shapes,
        in_specs=[pl.BlockSpec(memory_space=pltpu.HBM)] * 5,
        out_specs=(anyspace,) * 4,
        scratch_shapes=list(scratch.values()),
        compiler_params=pltpu.CompilerParams(
            collective_id=0, has_side_effects=True, vmem_limit_bytes=48 * 2**20
        ),
    )(*stay)
    out, grad, first, second = pl.pallas_call(
        hand_on,
        name="hand_on",
        out_shape=shapes,
        in_specs=[anyspace] * 4,
        out_specs=(anyspace,) * 4,
        scratch_shapes=[dma((4,))],
        compiler_params=pltpu.CompilerParams(vmem_limit_bytes=8 * 2**20),
    )(*results)
    return out.reshape(features.shape), grad.reshape(features.shape), first, second


def solution(mesh):
    in_specs = (P("gx", "gy", None, None), P(), P(), P("gx", "gy", None), P("gx", "gy", None, None))
    out_specs = (
        P("gx", "gy", None, None),
        P("gx", "gy", None, None),
        P(None, "gy", None),
        P(None, "gy", None),
    )
    return jax.shard_map(body, mesh=mesh, in_specs=in_specs, out_specs=out_specs, check_vma=False)
```
